256 devices in a mesh: order: 8 (over z_hi, core), blk: 32 (over y, x, z_lo).
Axes of the slice: x: 4, y: 4, z: 8 (z_hi: 4, z_lo: 2; z = z_hi * 2 + z_lo), core: 2. Of those that a mesh axis runs over, the one named last changes fastest.
Arguments:
- emode_coeffs: bfloat16 [4096, 32, 128], P('blk', 'order'), may hold values from -6 to 6
- lensing_coeffs: bfloat16 [4096, 32, 128], P('blk', 'order'), may hold values from -6 to 6
- order_values: int32 [32], replicated, may hold values from 0 to 4095, as said below
- circle_indices: int32 [4096], replicated, may hold values from 0 to 4095, each once
- circle_weights: float32 [4096], replicated, may hold values from 0.25 to 1
Outputs:
- gradient_part: bfloat16 [4096, 32, 128], P('blk', 'order')
- curl_part: bfloat16 [4096, 32, 128], P('blk', 'order')
The draws below stay inside these ranges and needn't reach their ends.
Inputs may be any that keep to these rules, and one draw needn't show every extreme that they name: `order_values`: distinct; exactly one value lies in each band from b * 128 to (b + 1) * 128 - 1. `circle_indices`: each circle of the sky exactly once.
All inputs are finite; a program needn't handle non-finite values.
Results may differ from the reference program's by a relative error of at most 0.012.
The reference program's roundings to bfloat16 on the way count: a program that leaves them out, or rounds other values in their place, can miss the bound.
Values may be sent and summed in bfloat16 or wider, within the bound.
No kernel may reach another device: no remote copies, remote signals or barrier semaphores. Data moves between devices by JAX's collectives and lax.ppermute only.
A program may use at most 128 MiB of HBM per device.

```python
import math
import jax
import jax.numpy as jnp
from jax import lax

LMAX = 4096
ORDERS = 32
CIRCLE_DEV = 128
CIRCLES = 4096
SIMS = 64
LONGS = 256


def draw_order_values(key, part):
    stride = LMAX // ORDERS
    band_index = jax.random.permutation(jax.random.fold_in(key, 11), ORDERS).astype(jnp.int32)
    within = jax.random.randint(jax.random.fold_in(key, 12), (ORDERS,), 0, stride).astype(jnp.int32)
    within = jnp.where(band_index == 0, 0, within)
    within = jnp.where(band_index == ORDERS - 1, stride - 1, within)
    return (band_index * stride + within).astype(jnp.int32)


def steps_of(stream_key, extent, cuts, low, top_value):
    loudness, own = 1.0, jax.random.fold_in(stream_key, 6)
    for axis_at, blocks in cuts:
        heights = jnp.exp(jax.random.uniform(jax.random.fold_in(own, axis_at), (blocks,), jnp.float32, low / len(cuts), top_value / len(cuts)))
        loudness = loudness * jnp.repeat(heights, extent[axis_at] // blocks).reshape([-1 if axis == axis_at else 1 for axis in range(len(extent))])
    return loudness


def gaussian(rng, dims, scale, bound, shards=(), held_as=jnp.bfloat16):
    values = scale * jax.random.normal(rng, dims, jnp.float32)
    if shards:
        values = values * steps_of(rng, dims, shards, -0.22, 0.18)
    return jnp.clip(values, -bound, bound).astype(held_as)


def setup_inputs(seed: int = 0) -> dict:
    keys = jax.random.split(jax.random.key(seed), 6)
    emode_coeffs = gaussian(keys[0], (LMAX, ORDERS, 2 * SIMS), 1.0, 6.0, ((0, 32), (1, 8)))
    lensing_coeffs = gaussian(keys[1], (LMAX, ORDERS, 2 * SIMS), 1.0, 6.0, ((0, 32), (1, 8)))
    order_values = draw_order_values(jax.random.fold_in(keys[5], 71), 0)
    circle_indices = jax.random.permutation(keys[3], CIRCLES).astype(jnp.int32)
    circle_weights = jnp.clip(jnp.exp(jax.random.uniform(keys[4], (CIRCLES,), jnp.float32, math.log(0.25), math.log(1.0))), 0.25, 1.0)
    return {"emode_coeffs": emode_coeffs, "lensing_coeffs": lensing_coeffs, "order_values": order_values, "circle_indices": circle_indices, "circle_weights": circle_weights}


def spin_tables(degrees, circle_list, order_list, spin_shift, circle_total):
    frequency = 2 * degrees + 1 + spin_shift
    colatitude = 2 * circle_list + 1
    phases = colatitude[None, :, None] * frequency[None, None, :] - 2 * circle_total * order_list[:, None, None]
    phases = jnp.mod(phases, 8 * circle_total)
    angles = phases.astype(jnp.float32) * (math.pi / (4 * circle_total))
    amplitude = math.sqrt(2.0 / LMAX)
    inside = degrees[None, None, :] >= order_list[:, None, None]
    cosine = jnp.where(inside, amplitude * jnp.cos(angles), 0.0)
    weight_deg = (frequency.astype(jnp.float32) / (2.0 * LMAX))[None, None, :]
    slopes = jnp.where(inside, -weight_deg * amplitude * jnp.sin(angles), 0.0)
    return (cosine.astype(jnp.bfloat16), slopes.astype(jnp.bfloat16))

def longitude_table(circle_list, order_list):
    full_circle = 2 * LMAX
    longitude = jnp.arange(LONGS, dtype=jnp.int32)
    parity = jnp.mod(circle_list, 2)
    phase_steps = order_list[None, :, None] * (2 * longitude[None, None, :] + parity[:, None, None])
    phase_steps = jnp.mod(phase_steps, 2 * full_circle)
    angles = phase_steps.astype(jnp.float32) * (math.pi / full_circle)
    scaling = 1.0 / math.sqrt(order_list.shape[0])
    fourier = jnp.concatenate([jnp.cos(angles) * scaling, -jnp.sin(angles) * scaling], axis=1)
    return fourier.astype(jnp.bfloat16)

def rotate(block, factor):
    return jnp.concatenate([-block[..., SIMS:], block[..., :SIMS]], axis=-1) * factor

def reference(emode_coeffs, lensing_coeffs, order_values, circle_indices, circle_weights):
    csims = 2 * SIMS
    degrees = jnp.arange(LMAX, dtype=jnp.int32)

    def synth_order(order_slot):
        order_one = lax.dynamic_slice_in_dim(order_values, order_slot, 1)
        emode = lax.dynamic_index_in_dim(emode_coeffs, order_slot, 1, keepdims=False)
        lens = lax.dynamic_index_in_dim(lensing_coeffs, order_slot, 1, keepdims=False)
        cos_plus, der_plus = spin_tables(degrees, circle_indices, order_one, 2, CIRCLES)
        cos_minus, der_minus = spin_tables(degrees, circle_indices, order_one, -2, CIRCLES)
        cos_zero, der_zero = spin_tables(degrees, circle_indices, order_one, 0, CIRCLES)
        factor = order_one[0].astype(jnp.float32) / LMAX
        q_theta = jnp.dot(der_plus[0], emode, preferred_element_type=jnp.float32)
        u_theta = jnp.dot(der_minus[0], emode, preferred_element_type=jnp.float32)
        q_cos = jnp.dot(cos_plus[0], emode, preferred_element_type=jnp.float32)
        u_cos = jnp.dot(cos_minus[0], emode, preferred_element_type=jnp.float32)
        d_theta = jnp.dot(der_zero[0], lens, preferred_element_type=jnp.float32)
        d_cos = jnp.dot(cos_zero[0], lens, preferred_element_type=jnp.float32)
        joined = jnp.concatenate([q_theta, u_theta, rotate(q_cos, factor), rotate(u_cos, factor), d_theta, rotate(d_cos, factor)], axis=-1)
        return joined.astype(jnp.bfloat16)
    modes = lax.map(synth_order, jnp.arange(ORDERS, dtype=jnp.int32))
    nblocks = CIRCLES // CIRCLE_DEV
    mode_blocks = modes.reshape(ORDERS, nblocks, CIRCLE_DEV, 6 * csims).transpose(1, 0, 2, 3)
    circle_blocks = circle_indices.reshape(nblocks, CIRCLE_DEV)
    weight_blocks = circle_weights.reshape(nblocks, CIRCLE_DEV)

    def pixel_block(operands):
        block_modes, block_circles, block_weights = operands
        arranged = block_modes.reshape(ORDERS, CIRCLE_DEV, 6, 2, SIMS).transpose(1, 3, 0, 2, 4)
        arranged = arranged.reshape(CIRCLE_DEV, 2 * ORDERS, 6 * SIMS)
        fourier = longitude_table(block_circles, order_values)
        pixels = jnp.einsum('knj,knc->kjc', fourier.astype(jnp.float32), arranged.astype(jnp.float32))
        pixels = pixels.reshape(CIRCLE_DEV, LONGS, 6, SIMS)
        delta_q = pixels[:, :, 4] * pixels[:, :, 0] + pixels[:, :, 5] * pixels[:, :, 2]
        delta_u = pixels[:, :, 4] * pixels[:, :, 1] + pixels[:, :, 5] * pixels[:, :, 3]
        deflected = jnp.concatenate([delta_q, delta_u], axis=-1).astype(jnp.bfloat16)
        analysed = jnp.einsum('knj,kjc->knc', fourier.astype(jnp.float32), deflected.astype(jnp.float32))
        weighted = (analysed * block_weights[:, None, None]).astype(jnp.bfloat16)
        weighted = weighted.reshape(CIRCLE_DEV, 2, ORDERS, 2, SIMS).transpose(0, 2, 3, 1, 4)
        return weighted.reshape(CIRCLE_DEV, ORDERS, 4 * SIMS)
    weighted_all = lax.map(pixel_block, (mode_blocks, circle_blocks, weight_blocks))
    weighted_all = weighted_all.reshape(CIRCLES, ORDERS, 4 * SIMS)

    def adjoint_order(order_slot):
        order_one = lax.dynamic_slice_in_dim(order_values, order_slot, 1)
        circle_maps = lax.dynamic_index_in_dim(weighted_all, order_slot, 1, keepdims=False)
        cos_plus, unused_plus = spin_tables(degrees, circle_indices, order_one, 2, CIRCLES)
        cos_minus, unused_minus = spin_tables(degrees, circle_indices, order_one, -2, CIRCLES)
        plus = jnp.dot(cos_plus[0].T, circle_maps, preferred_element_type=jnp.float32)
        minus = jnp.dot(cos_minus[0].T, circle_maps, preferred_element_type=jnp.float32)
        gradient = plus[:, :csims] + minus[:, csims:]
        curl = plus[:, csims:] - minus[:, :csims]
        return jnp.concatenate([gradient, curl], axis=-1)
    summed = lax.map(adjoint_order, jnp.arange(ORDERS, dtype=jnp.int32)).transpose(1, 0, 2)
    return (summed[..., :csims].astype(jnp.bfloat16), summed[..., csims:].astype(jnp.bfloat16))
```

```python
import math

import jax
import jax.numpy as jnp
import numpy as np
from jax import lax
from jax.experimental import pallas as pl
from jax.experimental.pallas import tpu as pltpu

LMAX = 4096
ORD_DEV = 4
SIMS = 64
LONGS = 256
SPINS = (2, -2, 0)
F32 = jnp.float32
BF16 = jnp.bfloat16


def split_hi_lo(values):
    values = values.astype(np.float32)
    hi = values.astype(jnp.bfloat16)
    lo = (values - hi.astype(np.float32)).astype(jnp.bfloat16)
    return hi, lo


def make_constants():
    a = np.arange(32)
    b = np.arange(128)
    c = np.arange(64)
    e = np.arange(32)
    amp = math.sqrt(2.0 / LMAX)
    first = np.pi * np.outer(2 * e + 1, a) / 64.0
    plain = np.concatenate([np.cos(first), np.sin(first)], axis=0)
    both = np.concatenate([plain, plain * (a / 32.0)[None, :]], axis=0)
    hi, lo = split_hi_lo(both)
    w1 = np.concatenate([hi, lo], axis=1)
    twiddle, w2, wadj = [], [], []
    for s in SPINS:
        f = 2 * b + 1 + s
        t = np.pi * np.outer(2 * e + 1, f) / 16384.0
        twiddle += [amp * np.cos(t), amp * np.sin(t)]
        at_c = np.pi * np.outer(f, c) / 128.0
        at_n = np.pi * np.outer(f, c + 1) / 128.0
        full = np.concatenate(
            [
                np.concatenate([np.cos(at_c), np.cos(at_n)], axis=1),
                np.concatenate([-np.sin(at_c), np.sin(at_n)], axis=1),
            ],
            axis=0,
        )
        w2.append(np.stack(split_hi_lo(full)))
        if s:
            back = np.concatenate([full[:128].T, -full[128:].T], axis=1)
            wadj.append(np.concatenate(split_hi_lo(back), axis=0))
    last = np.concatenate([np.cos(first).T, -np.sin(first).T], axis=1)
    hi, lo = split_hi_lo(last)
    w3 = np.concatenate([hi, hi, lo], axis=1)
    return {
        "w1": w1,
        "tw": np.stack(twiddle).astype(np.float32),
        "w2": np.stack(w2),
        "wadj": np.concatenate(wadj, axis=1),
        "w3": w3,
    }


CONST = make_constants()


def order_phase(m):
    q = jnp.bitwise_and(m, 3)
    pc = jnp.where(q == 0, 1.0, jnp.where(q == 2, -1.0, 0.0)).astype(F32)
    ps = jnp.where(q == 1, 1.0, jnp.where(q == 3, -1.0, 0.0)).astype(F32)
    sign = jnp.where(jnp.bitwise_and(m, 1) == 0, 1.0, -1.0).astype(F32)
    return pc, ps, sign


def half_sign(width, value):
    lane = lax.broadcasted_iota(jnp.int32, (1, width), 1)
    return jnp.where(jnp.bitwise_and(lane, 127) < 64, jnp.float32(1.0), value)


def degree_index():
    return lax.broadcasted_iota(jnp.int32, (32, 128), 0) * 128 + lax.broadcasted_iota(
        jnp.int32, (32, 128), 1
    )


def pack_kernel(e_ref, x_ref, out_ref, src, dst):
    for field, ref in enumerate((e_ref, x_ref)):
        src[...] = ref[...].astype(F32)
        for o in range(ORD_DEV):
            t = src[pl.ds(o, 128, stride=ORD_DEV), :].T
            for ri in range(2):
                for s in range(2):
                    j = o * 8 + field * 4 + ri * 2 + s
                    at = ri * 64 + s * 32
                    dst[pl.ds(j, 32, stride=32), :] = t[at : at + 32, :]
    out_ref[...] = dst[...].astype(BF16)


def unpack_kernel(in_ref, g_ref, c_ref, src, dst):
    src[...] = in_ref[...].astype(F32)
    for part, ref in enumerate((g_ref, c_ref)):
        for o in range(ORD_DEV):
            rows = []
            for ri in range(2):
                for s in range(2):
                    j = o * 8 + part * 4 + ri * 2 + s
                    rows.append(src[pl.ds(j, 32, stride=32), :])
            dst[pl.ds(o, 128, stride=ORD_DEV), :] = jnp.concatenate(rows, axis=0).T
        ref[...] = dst[...].astype(BF16)


def synth_kernel(m_ref, x_ref, w1_ref, tw_ref, w2_ref, out_ref, xs, os):
    xs[...] = x_ref[...].astype(F32)
    degree = degree_index()
    lane = lax.broadcasted_iota(jnp.int32, (1, 128), 1)
    for o in range(ORD_DEV):
        m = m_ref[o]
        inside = degree >= m
        pc, ps, sign = order_phase(m)
        factor = m.astype(F32) * (1.0 / LMAX)
        for field in range(2):
            tiles = []
            for t in range(4):
                j = o * 8 + field * 4 + t
                tile = xs[pl.ds(j, 32, stride=32), :]
                tiles.append(jnp.where(inside, tile, 0.0).astype(BF16))
            rhs = jnp.concatenate(tiles, axis=1)
            rhs = jnp.concatenate([rhs, rhs], axis=0)
            first = jnp.dot(w1_ref[...], rhs, preferred_element_type=F32)
            for k in (0, 1) if field == 0 else (2,):
                ar, ai = tw_ref[2 * k], tw_ref[2 * k + 1]
                tr = ar * pc + ai * ps
                ti = ai * pc - ar * ps
                slope = (2 * lane + 1 + SPINS[k]).astype(F32) * (1.0 / (2 * LMAX))
                rows_c, rows_d = [], []
                for t in range(4):
                    part = first[:, t * 128 : (t + 1) * 128]
                    sr, si = part[0:32], part[32:64]
                    vr = part[64:96] + slope * sr
                    vi = part[96:128] + slope * si
                    rows_c.append(jnp.concatenate([sr * tr - si * ti, sr * ti + si * tr], axis=1))
                    rows_d.append(
                        jnp.concatenate([-(vr * ti + vi * tr), vr * tr - vi * ti], axis=1)
                    )
                lhs = jnp.concatenate(rows_c + rows_d, axis=0)
                hi = lhs.astype(BF16)
                lo = (lhs - hi.astype(F32)).astype(BF16)
                y = (
                    jnp.dot(hi, w2_ref[k, 0], preferred_element_type=F32)
                    + jnp.dot(lo, w2_ref[k, 0], preferred_element_type=F32)
                    + jnp.dot(hi, w2_ref[k, 1], preferred_element_type=F32)
                )
                cos_sum = y[:128] * half_sign(128, sign)
                der_sum = y[128:] * half_sign(128, -sign)
                der_map, cos_map = ((0, 2), (1, 3), (4, 5))[k]
                for ri in range(2):
                    scale = -factor if ri == 0 else factor
                    for s in range(2):
                        t = ri * 2 + s
                        u = (1 - ri) * 2 + s
                        rows = pl.ds(o * 2 + ri, 32, stride=8)
                        os[der_map * 2 + s, rows, :] = der_sum[t * 32 : (t + 1) * 32]
                        os[cos_map * 2 + s, rows, :] = cos_sum[u * 32 : (u + 1) * 32] * scale
    for k in range(12):
        out_ref[:, k * 128 : (k + 1) * 128] = os[k].astype(BF16)


def pixel_kernel(x_ref, ft_ref, f_ref, w_ref, out_ref):
    lane_in = lax.broadcasted_iota(jnp.int32, (1, 12 * 128), 1)
    low_in = jnp.bitwise_and(lane_in, 127) < 64
    lane_out = lax.broadcasted_iota(jnp.int32, (1, 4 * 128), 1)
    low_out = jnp.bitwise_and(lane_out, 127) < 64

    def rows_of(i):
        chunks = [x_ref[g * 32 + i * 8 : g * 32 + i * 8 + 8, :].astype(F32) for g in range(8)]
        return jnp.concatenate(chunks, axis=0)

    for pair in range(2):
        i0, i1 = 2 * pair, 2 * pair + 1
        x0, x1 = rows_of(i0), rows_of(i1)
        results = []
        for parity in range(2):
            if parity == 0:
                x = jnp.where(low_in, x0, x1)
            else:
                x = jnp.where(low_in, x1, x0)
            px = jnp.dot(ft_ref[parity], x.astype(BF16), preferred_element_type=F32)
            qt, ut, qp, up, dt, dp = (px[:, k * 256 : (k + 1) * 256] for k in range(6))
            deflected = jnp.concatenate([dt * qt + dp * qp, dt * ut + dp * up], axis=1)
            results.append(
                jnp.dot(f_ref[parity], deflected.astype(BF16), preferred_element_type=F32)
            )
        even, odd = results
        for i, g in ((i0, jnp.where(low_out, even, odd)), (i1, jnp.where(low_out, odd, even))):
            w = w_ref[i : i + 1, :]
            g = (g * jnp.concatenate([w, w, w, w], axis=1)).astype(BF16)
            for k in range(8):
                out_ref[k * 32 + i * 8 : k * 32 + i * 8 + 8, :] = g[k * 8 : k * 8 + 8]


def adjoint_kernel(m_ref, g_ref, tw_ref, wadj_ref, w3_ref, out_ref, gs, os):
    for t in range(4):
        gs[t] = g_ref[:, t * 128 : (t + 1) * 128].astype(F32)
    degree = degree_index()
    for o in range(ORD_DEV):
        m = m_ref[o]
        inside = degree >= m
        pc, ps, sign = order_phase(m)
        signs = half_sign(128, sign)
        turned = []
        for k in range(2):
            ar, ai = tw_ref[2 * k], tw_ref[2 * k + 1]
            turned.append((ar * pc + ai * ps, ai * pc - ar * ps))
        (pr, pi), (mr, mi) = turned
        rows = []
        for ri in range(2):
            rows += [gs[t, pl.ds(o * 2 + ri, 32, stride=8), :] * signs for t in range(4)]
        lhs = jnp.concatenate(rows, axis=0).astype(BF16)
        lhs = jnp.concatenate([lhs, lhs], axis=1)
        y = jnp.dot(lhs, wadj_ref[...], preferred_element_type=F32)
        for ri in range(2):
            for s in range(2):
                yq = y[(ri * 4 + s) * 32 : (ri * 4 + s) * 32 + 32]
                yu = y[(ri * 4 + 2 + s) * 32 : (ri * 4 + 2 + s) * 32 + 32]
                qr, qi, nr, ni = (yq[:, t * 128 : (t + 1) * 128] for t in range(4))
                ur, ui, vr, vi = (yu[:, t * 128 : (t + 1) * 128] for t in range(4))
                grad_re = pr * qr - pi * qi + mr * vr - mi * vi
                grad_im = pr * qi + pi * qr + mr * vi + mi * vr
                curl_re = pr * ur - pi * ui - mr * nr + mi * ni
                curl_im = pr * ui + pi * ur - mr * ni - mi * nr
                p = jnp.concatenate(
                    [
                        jnp.concatenate([grad_re, curl_re], axis=1),
                        jnp.concatenate([grad_im, curl_im], axis=1),
                    ],
                    axis=0,
                )
                hi = p.astype(BF16)
                lo = (p - hi.astype(F32)).astype(BF16)
                rhs = jnp.concatenate([hi, lo, hi], axis=0)
                r = jnp.dot(w3_ref[...], rhs, preferred_element_type=F32)
                for part in range(2):
                    j = o * 8 + part * 4 + ri * 2 + s
                    value = jnp.where(inside, r[:, part * 128 : part * 128 + 128], 0.0)
                    os[pl.ds(j, 32, stride=32), :] = value
    out_ref[...] = os[...].astype(BF16)


VMEM = pl.BlockSpec(memory_space=pltpu.VMEM)
SMEM = pl.BlockSpec(memory_space=pltpu.SMEM)


def call(kernel, name, inputs, out_shapes, scratch):
    specs = [SMEM if x.ndim == 1 else VMEM for x in inputs]
    single = len(out_shapes) == 1
    out = pl.pallas_call(
        kernel,
        name=name,
        out_shape=[jax.ShapeDtypeStruct(s, BF16) for s in out_shapes],
        in_specs=specs,
        out_specs=[VMEM for s in out_shapes],
        scratch_shapes=[pltpu.VMEM(s, F32) for s in scratch],
        compiler_params=pltpu.CompilerParams(vmem_limit_bytes=48 << 20),
    )(*inputs)
    return out[0] if single else out


def fourier_tables(order_values):
    longitude = jnp.arange(LONGS, dtype=jnp.int32)
    full_circle = 2 * LMAX
    parity = jnp.arange(2, dtype=jnp.int32)
    steps = order_values[None, :, None] * (2 * longitude[None, None, :] + parity[:, None, None])
    steps = jnp.mod(steps, 2 * full_circle)
    angles = steps.astype(F32) * (math.pi / full_circle)
    scaling = 1.0 / math.sqrt(order_values.shape[0])
    f = jnp.stack([jnp.cos(angles) * scaling, -jnp.sin(angles) * scaling], axis=2)
    f = f.astype(BF16).reshape(2, 2 * order_values.shape[0], LONGS)
    return f, f.transpose(0, 2, 1)


def weights_by_circle(circle_indices, circle_weights, order_pos):
    e = order_pos * 4 + jnp.arange(4, dtype=jnp.int32)
    ds = jnp.concatenate([e, 63 - e])
    low = jnp.bitwise_and(circle_indices, 63)
    high = jnp.right_shift(circle_indices, 6)
    picked = jnp.where(low[None, :] == ds[:, None], circle_weights[None, :], 0.0)
    chosen = (high[:, None] == jnp.arange(64, dtype=jnp.int32)[None, :]).astype(F32)
    w = jnp.dot(picked, chosen, precision=lax.Precision.HIGHEST)
    return jnp.concatenate([w[:4], w[4:]], axis=1)


def body(emode_coeffs, lensing_coeffs, order_values, circle_indices, circle_weights):
    order_pos = lax.axis_index("order")
    my_orders = lax.dynamic_slice_in_dim(order_values, order_pos * ORD_DEV, ORD_DEV)
    const = {k: jnp.asarray(v) for k, v in CONST.items()}
    fourier, fourier_t = fourier_tables(order_values)
    weights = weights_by_circle(circle_indices, circle_weights, order_pos)
    sent = call(
        pack_kernel,
        "pack",
        [emode_coeffs.reshape(512, 128), lensing_coeffs.reshape(512, 128)],
        [(1024, 128)],
        [(512, 128), (1024, 128)],
    )
    got = lax.all_to_all(sent.reshape(32, 32, 128), "blk", 0, 0, tiled=True)
    modes = call(
        synth_kernel,
        "synth",
        [my_orders, got.reshape(1024, 128), const["w1"], const["tw"], const["w2"]],
        [(256, 1536)],
        [(1024, 128), (12, 256, 128)],
    )
    spread = lax.all_to_all(modes.reshape(8, 32, 1536), "order", 0, 0, tiled=True)
    weighted = call(
        pixel_kernel,
        "pixel",
        [spread.reshape(256, 1536), fourier_t, fourier, weights],
        [(256, 512)],
        [],
    )
    back = lax.all_to_all(weighted.reshape(8, 32, 512), "order", 0, 0, tiled=True)
    sums = call(
        adjoint_kernel,
        "adjoint",
        [my_orders, back.reshape(256, 512), const["tw"], const["wadj"], const["w3"]],
        [(1024, 128)],
        [(4, 256, 128), (1024, 128)],
    )
    home = lax.all_to_all(sums.reshape(32, 32, 128), "blk", 0, 0, tiled=True)
    grad, curl = call(
        unpack_kernel,
        "unpack",
        [home.reshape(1024, 128)],
        [(512, 128), (512, 128)],
        [(1024, 128), (512, 128)],
    )
    return grad.reshape(128, ORD_DEV, 128), curl.reshape(128, ORD_DEV, 128)


def solution(mesh):
    from jax.sharding import PartitionSpec as P

    placed = (P("blk", "order", None), P("blk", "order", None), P(), P(), P())
    return jax.shard_map(
        body,
        mesh=mesh,
        in_specs=placed,
        out_specs=(P("blk", "order", None), P("blk", "order", None)),
        check_vma=False,
    )
```

```python
import math

import jax
import jax.numpy as jnp
import numpy as np
from jax import lax
from jax.experimental import pallas as pl
from jax.experimental.pallas import tpu as pltpu
from jax.sharding import Mesh
from jax.sharding import PartitionSpec as P

LMAX = 4096
ORD_DEV = 4
ORD_ROW = 8
SIMS = 64
LONGS = 256
SPINS = (2, -2, 0)
ALL = ("row", "core", "y", "x", "z")


def quad_position():
    return jnp.where(lax.axis_index("core") == 0, lax.axis_index("y"), lax.axis_index("x"))


def quad_shift(shift):
    pairs = []
    for row, core, y, x, z in np.ndindex(4, 2, 4, 4, 2):
        to = (row, core, (y + shift) % 4, x, z) if core == 0 else (row, core, y, (x + shift) % 4, z)
        dims = (4, 2, 4, 4, 2)
        pairs.append(
            (int(np.ravel_multi_index((row, core, y, x, z), dims)), int(np.ravel_multi_index(to, dims)))
        )
    return pairs


def exchange(blocks, direction):
    return [blocks[0]] + [
        lax.ppermute(blocks[k], ALL, quad_shift(direction * k)) for k in (1, 2, 3)
    ]


def realization_rows(o):
    out = []
    for row in range(4):
        out.append(((row * 64 + o * 8) * 4, 8, 4, row * 16))
        for z in range(2):
            out.append(((row * 64 + 32 + o * 2 + z) * 4, 4, 32, row * 16 + 8 + z * 4))
    return out
F32 = jnp.float32
BF16 = jnp.bfloat16


def split_hi_lo(values):
    values = values.astype(np.float32)
    hi = values.astype(jnp.bfloat16)
    lo = (values - hi.astype(np.float32)).astype(jnp.bfloat16)
    return hi, lo


def make_constants():
    a = np.arange(32)
    b = np.arange(128)
    c = np.arange(64)
    e = np.arange(32)
    amp = math.sqrt(2.0 / LMAX)
    first = np.pi * np.outer(2 * e + 1, a) / 64.0
    plain = np.concatenate([np.cos(first), np.sin(first)], axis=0)
    both = np.concatenate([plain, plain * (a / 32.0)[None, :]], axis=0)
    hi, lo = split_hi_lo(both)
    w1 = np.concatenate([hi, lo], axis=1)
    twiddle, w2, wadj = [], [], []
    for s in SPINS:
        f = 2 * b + 1 + s
        t = np.pi * np.outer(2 * e + 1, f) / 16384.0
        twiddle += [amp * np.cos(t), amp * np.sin(t)]
        at_c = np.pi * np.outer(f, c) / 128.0
        at_n = np.pi * np.outer(f, c + 1) / 128.0
        full = np.concatenate(
            [
                np.concatenate([np.cos(at_c), np.cos(at_n)], axis=1),
                np.concatenate([-np.sin(at_c), np.sin(at_n)], axis=1),
            ],
            axis=0,
        )
        w2.append(np.concatenate(split_hi_lo(full), axis=1))
        if s:
            back = np.concatenate([full[:128].T, -full[128:].T], axis=1)
            wadj.append(np.concatenate(split_hi_lo(back), axis=0))
    last = np.concatenate([np.cos(first).T, -np.sin(first).T], axis=1)
    hi, lo = split_hi_lo(last)
    w3 = np.concatenate([hi, hi, lo], axis=1)
    return {
        "w1": w1,
        "tw": np.stack(twiddle).astype(np.float32),
        "w2": np.stack(w2),
        "wadj": np.concatenate(wadj, axis=1),
        "w3": w3,
    }


CONST = make_constants()


def order_phase(m):
    q = jnp.bitwise_and(m, 3)
    pc = jnp.where(q == 0, 1.0, jnp.where(q == 2, -1.0, 0.0)).astype(F32)
    ps = jnp.where(q == 1, 1.0, jnp.where(q == 3, -1.0, 0.0)).astype(F32)
    sign = jnp.where(jnp.bitwise_and(m, 1) == 0, 1.0, -1.0).astype(F32)
    return pc, ps, sign


def half_sign(width, value):
    lane = lax.broadcasted_iota(jnp.int32, (1, width), 1)
    return jnp.where(jnp.bitwise_and(lane, 127) < 64, jnp.float32(1.0), value)


def degree_index():
    return lax.broadcasted_iota(jnp.int32, (32, 128), 0) * 128 + lax.broadcasted_iota(
        jnp.int32, (32, 128), 1
    )


def fourier_tables(m_ref, t, f_ref):
    row = lax.broadcasted_iota(jnp.int32, (64, LONGS), 0)
    longitude = lax.broadcasted_iota(jnp.int32, (64, LONGS), 1)
    slot = jnp.right_shift(row, 1)
    m = jnp.zeros((64, LONGS), jnp.int32)
    for k in range(32):
        value = m_ref[4 * (k % 8) + jnp.bitwise_and(t - k // 8, 3)]
        m = jnp.where(slot == k, value, m)
    quarter = jnp.bitwise_and(row, 1) * LMAX
    for parity in range(2):
        steps = jnp.bitwise_and(m * (2 * longitude + parity) + quarter, 4 * LMAX - 1)
        angles = steps.astype(F32) * (math.pi / (2 * LMAX))
        f_ref[parity] = (jnp.cos(angles) * (1.0 / math.sqrt(32))).astype(BF16)


def weight_rows(row_pos, ci_ref, cw_ref, w_ref):
    e = lax.broadcasted_iota(jnp.int32, (16, 128), 0)
    ds = jnp.where(e < 8, row_pos * 8 + e, 71 - row_pos * 8 - e)
    cs = lax.broadcasted_iota(jnp.int32, (64, 128), 0)
    picked, chosen = [], []
    for k in range(32):
        circle = ci_ref[k : k + 1, :]
        low = jnp.bitwise_and(circle, 63)
        high = jnp.right_shift(circle, 6)
        chosen.append(jnp.where(high == cs, 1.0, 0.0).astype(BF16))
        w = jnp.where(low == ds, cw_ref[k : k + 1, :], 0.0)
        w_hi = w.astype(BF16)
        rest = w - w_hi.astype(F32)
        w_mid = rest.astype(BF16)
        w_lo = (rest - w_mid.astype(F32)).astype(BF16)
        picked.append(jnp.concatenate([w_hi, w_mid, w_lo], axis=0))
    w = lax.dot_general(
        jnp.concatenate(picked, axis=1),
        jnp.concatenate(chosen, axis=1),
        (((1,), (1,)), ((), ())),
        preferred_element_type=F32,
    )
    w = (w[32:] + w[16:32]) + w[:16]
    w_ref[...] = jnp.concatenate([w[:8], w[8:]], axis=1)


def pack_kernel(e_hbm, x_hbm, ci_hbm, cw_hbm, m_hbm, *refs):
    out_ref, f_ref, w_ref, ex, ci_ref, cw_ref, m_ref, src, dst, sems = refs
    copies = [
        pltpu.make_async_copy(e_hbm, ex.at[0], sems.at[0]),
        pltpu.make_async_copy(x_hbm, ex.at[1], sems.at[1]),
        pltpu.make_async_copy(ci_hbm, ci_ref, sems.at[2]),
        pltpu.make_async_copy(cw_hbm, cw_ref, sems.at[3]),
        pltpu.make_async_copy(m_hbm, m_ref, sems.at[4]),
    ]
    for copy in copies:
        copy.start()
    t = quad_position()
    copies[4].wait()
    fourier_tables(m_ref, t, f_ref)
    copies[2].wait()
    copies[3].wait()
    weight_rows(t, ci_ref, cw_ref, w_ref)
    for field in range(2):
        copies[field].wait()
        src[field] = ex[field].astype(F32)
        for o in range(ORD_DEV):
            tile = src[field, pl.ds(o, 128, stride=ORD_DEV), :].T
            for ri in range(2):
                j = field * 2 + ri
                for at, rows, stride, sim in realization_rows(o):
                    sim += ri * 64
                    dst[pl.ds(at + j, rows, stride=stride), :] = tile[sim : sim + rows, :]
    out_ref[...] = dst[...].astype(BF16)


def unpack_kernel(in_ref, g_ref, c_ref, src, dst):
    src[...] = in_ref[...].astype(F32)
    for part, ref in enumerate((g_ref, c_ref)):
        for o in range(ORD_DEV):
            rows = []
            for ri in range(2):
                j = part * 2 + ri
                for at, n, stride, sim in realization_rows(o):
                    rows.append(src[pl.ds(at + j, n, stride=stride), :])
            dst[part, pl.ds(o, 128, stride=ORD_DEV), :] = jnp.concatenate(rows, axis=0).T
        ref[...] = dst[part].astype(BF16)


def synth_kernel(m_ref, x_ref, w1_ref, tw_ref, w2_ref, *refs):
    out_refs, (xs, lhs_ref, os) = refs[:4], refs[4:]
    t = quad_position()
    xs[...] = x_ref[...].astype(F32)
    degree = degree_index()
    lane = lax.broadcasted_iota(jnp.int32, (1, 128), 1)
    for o in range(ORD_ROW):
        m = m_ref[4 * o + t]
        inside = degree >= m
        pc, ps, sign = order_phase(m)
        for field in range(2):
            tiles = []
            for ri in range(2):
                j = o * 128 + field * 2 + ri
                tile = xs[pl.ds(j, 32, stride=4), :]
                tiles.append(jnp.where(inside, tile, 0.0).astype(BF16))
            rhs = jnp.concatenate(tiles, axis=1)
            rhs = jnp.concatenate([rhs, rhs], axis=0)
            first = jnp.dot(w1_ref[...], rhs, preferred_element_type=F32)
            for k in (0, 1) if field == 0 else (2,):
                ar, ai = tw_ref[2 * k], tw_ref[2 * k + 1]
                tr = ar * pc + ai * ps
                ti = ai * pc - ar * ps
                slope = (2 * lane + 1 + SPINS[k]).astype(F32) * (1.0 / (2 * LMAX))
                for ri in range(2):
                    part = first[:, ri * 128 : (ri + 1) * 128]
                    sr, si = part[0:32], part[32:64]
                    vr = part[64:96] + slope * sr
                    vi = part[96:128] + slope * si
                    rows = (
                        (sr * tr - si * ti, sr * ti + si * tr),
                        (-(vr * ti + vi * tr), vr * tr - vi * ti),
                    )
                    for kind in range(2):
                        row = jnp.concatenate(rows[kind], axis=1)
                        hi = row.astype(BF16)
                        lo = (row - hi.astype(F32)).astype(BF16)
                        at = ((kind * ORD_ROW + o) * 2 + ri) * 32
                        lhs_ref[k, at : at + 32, :] = hi
                        lhs_ref[k, 1024 + at : 1024 + at + 32, :] = lo
    for k in range(3):
        y = jnp.dot(lhs_ref[k], w2_ref[k], preferred_element_type=F32)
        y = (y[1024:, :128] + y[:1024, 128:]) + y[:1024, :128]
        der_map, cos_map = ((0, 2), (1, 3), (4, 5))[k]
        for o in range(ORD_ROW):
            m = m_ref[4 * o + t]
            pc, ps, sign = order_phase(m)
            factor = m.astype(F32) * (1.0 / LMAX)
            for ri in range(2):
                rows = pl.ds(o * 2 + ri, 32, stride=16)
                scale = -factor if ri == 0 else factor
                at = (o * 2 + 1 - ri) * 32
                os[cos_map, rows, :] = y[at : at + 32] * (half_sign(128, sign) * scale)
                at = ((ORD_ROW + o) * 2 + ri) * 32
                os[der_map, rows, :] = y[at : at + 32] * half_sign(128, -sign)
    for shift in range(4):
        rows = pl.ds(jnp.bitwise_and(t + shift, 3) * 128, 128)
        for k in range(6):
            out_refs[shift][:, k * 128 : (k + 1) * 128] = os[k, rows, :].astype(BF16)


def pixel_kernel(*refs):
    x_refs, (f_ref, w_ref), out_refs = refs[:4], refs[4:6], refs[6:]
    low_in = lax.bitwise_and(lax.broadcasted_iota(jnp.int32, (1, 6 * 128), 1), 127) < 64
    low_out = lax.bitwise_and(lax.broadcasted_iota(jnp.int32, (1, 2 * 128), 1), 127) < 64

    def rows_of(i):
        chunks = [x_ref[i * 16 : i * 16 + 16, :] for x_ref in x_refs]
        return jnp.concatenate(chunks, axis=0).astype(F32)

    for pair in range(4):
        i0, i1 = 2 * pair, 2 * pair + 1
        x0, x1 = rows_of(i0), rows_of(i1)
        results = []
        for parity in range(2):
            if parity == 0:
                x = jnp.where(low_in, x0, x1)
            else:
                x = jnp.where(low_in, x1, x0)
            px = lax.dot_general(
                f_ref[parity],
                x.astype(BF16),
                (((0,), (0,)), ((), ())),
                preferred_element_type=F32,
            )
            qt, ut, qp, up, dt, dp = (px[:, k * 128 : (k + 1) * 128] for k in range(6))
            deflected = jnp.concatenate([dt * qt + dp * qp, dt * ut + dp * up], axis=1)
            results.append(
                jnp.dot(f_ref[parity], deflected.astype(BF16), preferred_element_type=F32)
            )
        even, odd = results
        for i, g in ((i0, jnp.where(low_out, even, odd)), (i1, jnp.where(low_out, odd, even))):
            w = w_ref[i : i + 1, :]
            g = (g * jnp.concatenate([w, w], axis=1)).astype(BF16)
            for k in range(4):
                out_refs[k][i * 16 : i * 16 + 16, :] = g[k * 16 : k * 16 + 16]


def adjoint_kernel(m_ref, *refs):
    g_refs, (tw_ref, wadj_ref, w3_ref, out_ref, gs, os) = refs[:4], refs[4:]
    t = quad_position()
    for shift in range(4):
        at = pl.ds(jnp.bitwise_and(t + shift, 3) * 128, 128)
        for k in range(2):
            gs[k, at, :] = g_refs[shift][:, k * 128 : (k + 1) * 128].astype(F32)
    degree = degree_index()
    rows = []
    for o in range(ORD_ROW):
        pc, ps, sign = order_phase(m_ref[4 * o + t])
        signs = half_sign(128, sign)
        for ri in range(2):
            rows += [gs[k, pl.ds(o * 2 + ri, 32, stride=16), :] * signs for k in range(2)]
    lhs = jnp.concatenate(rows, axis=0).astype(BF16)
    lhs = jnp.concatenate([lhs, lhs], axis=1)
    y = jnp.dot(lhs, wadj_ref[...], preferred_element_type=F32)
    for o in range(ORD_ROW):
        m = m_ref[4 * o + t]
        inside = degree >= m
        pc, ps, sign = order_phase(m)
        turned = []
        for k in range(2):
            ar, ai = tw_ref[2 * k], tw_ref[2 * k + 1]
            turned.append((ar * pc + ai * ps, ai * pc - ar * ps))
        (pr, pi), (mr, mi) = turned
        for ri in range(2):
            at = (o * 2 + ri) * 64
            yq, yu = y[at : at + 32], y[at + 32 : at + 64]
            qr, qi, nr, ni = (yq[:, k * 128 : (k + 1) * 128] for k in range(4))
            ur, ui, vr, vi = (yu[:, k * 128 : (k + 1) * 128] for k in range(4))
            grad_re = pr * qr - pi * qi + mr * vr - mi * vi
            grad_im = pr * qi + pi * qr + mr * vi + mi * vr
            curl_re = pr * ur - pi * ui - mr * nr + mi * ni
            curl_im = pr * ui + pi * ur - mr * ni - mi * nr
            p = jnp.concatenate(
                [
                    jnp.concatenate([grad_re, curl_re], axis=1),
                    jnp.concatenate([grad_im, curl_im], axis=1),
                ],
                axis=0,
            )
            hi = p.astype(BF16)
            lo = (p - hi.astype(F32)).astype(BF16)
            rhs = jnp.concatenate([hi, lo, hi], axis=0)
            r = jnp.dot(w3_ref[...], rhs, preferred_element_type=F32)
            for part in range(2):
                value = jnp.where(inside, r[:, part * 128 : part * 128 + 128], 0.0)
                os[pl.ds(o * 128 + part * 2 + ri, 32, stride=4), :] = value
    out_ref[...] = os[...].astype(BF16)


VMEM = pl.BlockSpec(memory_space=pltpu.VMEM)
SMEM = pl.BlockSpec(memory_space=pltpu.SMEM)
HBM = pl.BlockSpec(memory_space=pltpu.HBM)


def call(kernel, name, inputs, outs, scratch, spaces=None):
    specs = spaces or [SMEM if x.ndim == 1 else VMEM for x in inputs]
    single = len(outs) == 1
    out = pl.pallas_call(
        kernel,
        name=name,
        out_shape=[jax.ShapeDtypeStruct(s, d) for s, d in outs],
        in_specs=specs,
        out_specs=[VMEM for o in outs],
        scratch_shapes=scratch,
        compiler_params=pltpu.CompilerParams(vmem_limit_bytes=48 << 20),
    )(*inputs)
    return out[0] if single else out


def in_hbm(x):
    return pltpu.with_memory_space_constraint(x, pltpu.HBM)


def scratch(shape, dtype=F32):
    return pltpu.VMEM(shape, dtype)


def body(emode_coeffs, lensing_coeffs, order_values, circle_indices, circle_weights):
    const = {k: jnp.asarray(v) for k, v in CONST.items()}
    sent, fourier, weights = call(
        pack_kernel,
        "pack",
        [
            in_hbm(emode_coeffs.reshape(512, 128)),
            in_hbm(lensing_coeffs.reshape(512, 128)),
            in_hbm(circle_indices.reshape(32, 128)),
            in_hbm(circle_weights.reshape(32, 128)),
            in_hbm(order_values),
        ],
        [((1024, 128), BF16), ((2, 64, LONGS), BF16), ((8, 128), F32)],
        [
            scratch((2, 512, 128), BF16),
            scratch((32, 128), jnp.int32),
            scratch((32, 128), F32),
            pltpu.SMEM((32,), jnp.int32),
            scratch((2, 512, 128)),
            scratch((1024, 128)),
            pltpu.SemaphoreType.DMA((5,)),
        ],
        [HBM] * 5,
    )
    got = lax.all_to_all(sent.reshape(256, 4, 128), ALL, 0, 0, tiled=True)
    modes = call(
        synth_kernel,
        "synth",
        [order_values, got.reshape(1024, 128), const["w1"], const["tw"], const["w2"]],
        [((128, 768), BF16)] * 4,
        [scratch((1024, 128)), scratch((3, 2048, 256), BF16), scratch((6, 512, 128))],
    )
    weighted = call(
        pixel_kernel,
        "pixel",
        [*exchange(modes, 1), fourier, weights],
        [((128, 256), BF16)] * 4,
        [],
    )
    sums = call(
        adjoint_kernel,
        "adjoint",
        [order_values, *exchange(weighted, -1), const["tw"], const["wadj"], const["w3"]],
        [((1024, 128), BF16)],
        [scratch((2, 512, 128)), scratch((1024, 128))],
    )
    home = lax.all_to_all(sums.reshape(256, 4, 128), ALL, 0, 0, tiled=True)
    grad, curl = call(
        unpack_kernel,
        "unpack",
        [home.reshape(1024, 128)],
        [((512, 128), BF16), ((512, 128), BF16)],
        [scratch((1024, 128)), scratch((2, 512, 128))],
    )
    return grad.reshape(128, ORD_DEV, 128), curl.reshape(128, ORD_DEV, 128)


def solution(mesh):
    split = Mesh(mesh.devices.reshape(4, 2, 4, 4, 2), ALL)
    placed = P(("y", "x", "z"), ("row", "core"), None)
    return jax.shard_map(
        body,
        mesh=split,
        in_specs=(placed, placed, P(), P(), P()),
        out_specs=(placed, placed),
        check_vma=False,
    )
```

```python
import math

import jax
import jax.numpy as jnp
import numpy as np
from jax import lax
from jax.experimental import pallas as pl
from jax.experimental.pallas import tpu as pltpu
from jax.sharding import Mesh
from jax.sharding import PartitionSpec as P

LMAX = 4096
ORD_DEV = 4
ORD_ROW = 16
SIMS = 64
LONGS = 256
SPINS = (2, -2, 0)
ALL = ("row", "core", "y", "x", "z")


CHIPS = ("row", "y", "x", "z")


def place():
    return jnp.right_shift(lax.axis_index("row"), 1), lax.axis_index("core")


def order_slot(o, core):
    return (o // ORD_DEV) * 2 * ORD_DEV + core * ORD_DEV + o % ORD_DEV


def swap_cores(x):
    return lax.ppermute(x, "core", [(0, 1), (1, 0)])


F32 = jnp.float32
BF16 = jnp.bfloat16


def split_hi_lo(values):
    values = values.astype(np.float32)
    hi = values.astype(jnp.bfloat16)
    lo = (values - hi.astype(np.float32)).astype(jnp.bfloat16)
    return hi, lo


def make_constants():
    a = np.arange(32)
    b = np.arange(128)
    c = np.arange(64)
    e = np.arange(32)
    amp = math.sqrt(2.0 / LMAX)
    first = np.pi * np.outer(2 * e + 1, a) / 64.0
    plain = np.concatenate([np.cos(first), np.sin(first)], axis=0)
    both = np.concatenate([plain, plain * (a / 32.0)[None, :]], axis=0)
    hi, lo = split_hi_lo(both)
    w1 = np.concatenate([hi, lo], axis=1).reshape(4, 2, 16, 64)
    w1 = w1.transpose(1, 0, 2, 3).reshape(2, 64, 64)
    twiddle, w2, wadj = [], [], []
    for s in SPINS:
        f = 2 * b + 1 + s
        t = np.pi * np.outer(2 * e + 1, f) / 16384.0
        twiddle += [amp * np.cos(t), amp * np.sin(t)]
        at_c = np.pi * np.outer(f, c) / 128.0
        at_n = np.pi * np.outer(f, c + 1) / 128.0
        full = np.concatenate(
            [
                np.concatenate([np.cos(at_c), np.cos(at_n)], axis=1),
                np.concatenate([-np.sin(at_c), np.sin(at_n)], axis=1),
            ],
            axis=0,
        )
        w2.append(np.concatenate(split_hi_lo(full), axis=1))
        if s:
            back = np.concatenate([full[:128].T, -full[128:].T], axis=1)
            wadj.append(np.concatenate(split_hi_lo(back), axis=0))
    last = np.stack([np.cos(first).T, -np.sin(first).T], axis=1).reshape(32, 2, 2, 16)
    hi, lo = split_hi_lo(last.transpose(2, 0, 1, 3).reshape(2, 32, 32))
    w3 = np.concatenate([hi, hi, lo], axis=2)
    return {
        "w1": w1,
        "tw": np.stack(twiddle).astype(np.float32),
        "w2": np.stack(w2),
        "wadj": np.concatenate(wadj, axis=1),
        "w3": w3,
    }


CONST = make_constants()


def order_phase(m):
    q = jnp.bitwise_and(m, 3)
    pc = jnp.where(q == 0, 1.0, jnp.where(q == 2, -1.0, 0.0)).astype(F32)
    ps = jnp.where(q == 1, 1.0, jnp.where(q == 3, -1.0, 0.0)).astype(F32)
    sign = jnp.where(jnp.bitwise_and(m, 1) == 0, 1.0, -1.0).astype(F32)
    return pc, ps, sign


def half_sign(width, value):
    lane = lax.broadcasted_iota(jnp.int32, (1, width), 1)
    return jnp.where(jnp.bitwise_and(lane, 127) < 64, jnp.float32(1.0), value)


def degree_index():
    return lax.broadcasted_iota(jnp.int32, (32, 128), 0) * 128 + lax.broadcasted_iota(
        jnp.int32, (32, 128), 1
    )


def fourier_tables(m_ref, core, f_ref, ft_ref):
    row = lax.broadcasted_iota(jnp.int32, (64, LONGS), 0)
    longitude = lax.broadcasted_iota(jnp.int32, (64, LONGS), 1)
    slot = jnp.right_shift(row, 1)
    m = jnp.zeros((64, LONGS), jnp.int32)
    for k in range(32):
        value = m_ref[order_slot(k % 16, core if k < 16 else 1 - core)]
        m = jnp.where(slot == k, value, m)
    quarter = jnp.bitwise_and(row, 1) * LMAX
    for parity in range(2):
        steps = jnp.bitwise_and(m * (2 * longitude + parity) + quarter, 4 * LMAX - 1)
        angles = steps.astype(F32) * (math.pi / (2 * LMAX))
        table = jnp.cos(angles) * (1.0 / math.sqrt(32))
        f_ref[parity] = table.astype(BF16)
        ft_ref[parity] = table.T.astype(BF16)


def weight_rows(row_pos, ci_ref, cw_ref, w_ref):
    e = lax.broadcasted_iota(jnp.int32, (16, 128), 0)
    ds = jnp.where(e < 8, row_pos * 8 + e, 71 - row_pos * 8 - e)
    cs = lax.broadcasted_iota(jnp.int32, (64, 128), 0)
    picked, chosen = [], []
    for k in range(32):
        circle = ci_ref[k : k + 1, :]
        low = jnp.bitwise_and(circle, 63)
        high = jnp.right_shift(circle, 6)
        chosen.append(jnp.where(high == cs, 1.0, 0.0).astype(BF16))
        w = jnp.where(low == ds, cw_ref[k : k + 1, :], 0.0)
        w_hi = w.astype(BF16)
        rest = w - w_hi.astype(F32)
        w_mid = rest.astype(BF16)
        w_lo = (rest - w_mid.astype(F32)).astype(BF16)
        picked.append(jnp.concatenate([w_hi, w_mid, w_lo], axis=0))
    w = lax.dot_general(
        jnp.concatenate(picked, axis=1),
        jnp.concatenate(chosen, axis=1),
        (((1,), (1,)), ((), ())),
        preferred_element_type=F32,
    )
    w = (w[32:] + w[16:32]) + w[:16]
    w_ref[...] = jnp.concatenate([w[:8], w[8:]], axis=1)


def table_kernel(m_ref, ci_ref, cw_ref, f_ref, ft_ref, w_ref):
    half, core = place()
    fourier_tables(m_ref, core, f_ref, ft_ref)
    weight_rows(2 * half + core, ci_ref, cw_ref, w_ref)


def pack_kernel(e_hbm, x_hbm, m_hbm, out_ref, m_ref, ex, src, dst, sems):
    copies = [
        pltpu.make_async_copy(e_hbm, ex.at[0], sems.at[0]),
        pltpu.make_async_copy(x_hbm, ex.at[1], sems.at[1]),
        pltpu.make_async_copy(m_hbm, m_ref, sems.at[2]),
    ]
    for copy in copies:
        copy.start()
    for field in range(2):
        copies[field].wait()
        src[field] = ex[field].astype(F32)
        for o in range(ORD_DEV):
            tile = src[field, pl.ds(o, 128, stride=ORD_DEV), :].T
            for ri in range(2):
                j = o * 4 + field * 2 + ri
                dst[pl.ds(j, 64, stride=16), :] = tile[ri * 64 : ri * 64 + 64, :]
    packed = dst[...].astype(BF16)
    out_ref[:1024] = packed
    out_ref[1024:] = packed
    copies[2].wait()


def unpack_kernel(in_ref, g_ref, c_ref, src, dst):
    src[...] = in_ref[:1024].astype(F32) + in_ref[1024:].astype(F32)
    for part, ref in enumerate((g_ref, c_ref)):
        for o in range(ORD_DEV):
            rows = []
            for ri in range(2):
                j = o * 4 + part * 2 + ri
                rows.append(src[pl.ds(j, 64, stride=16), :])
            dst[part, pl.ds(o, 128, stride=ORD_DEV), :] = jnp.concatenate(rows, axis=0).T
        ref[...] = dst[part].astype(BF16)


def synth_kernel(m_ref, x_ref, w1_ref, tw_ref, w2_ref, *refs):
    keep_ref, send_ref, xs, lhs_ref, os = refs
    half, core = place()
    mine = pl.ds(half * 16, 16)
    xs[...] = x_ref[...].astype(F32)
    degree = degree_index()
    lane = lax.broadcasted_iota(jnp.int32, (1, 128), 1)
    for o in range(ORD_ROW):
        m = m_ref[order_slot(o, core)]
        inside = degree >= m
        pc, ps, sign = order_phase(m)
        for field in range(2):
            tiles = []
            for ri in range(2):
                j = (o // 4) * 512 + (o % 4) * 4 + field * 2 + ri
                tile = xs[pl.ds(j, 32, stride=16), :]
                tiles.append(jnp.where(inside, tile, 0.0).astype(BF16))
            rhs = jnp.concatenate(tiles, axis=1)
            rhs = jnp.concatenate([rhs, rhs], axis=0)
            first = jnp.dot(w1_ref[half], rhs, preferred_element_type=F32)
            for k in (0, 1) if field == 0 else (2,):
                ar, ai = tw_ref[2 * k, mine, :], tw_ref[2 * k + 1, mine, :]
                tr = ar * pc + ai * ps
                ti = ai * pc - ar * ps
                slope = (2 * lane + 1 + SPINS[k]).astype(F32) * (1.0 / (2 * LMAX))
                for ri in range(2):
                    part = first[:, ri * 128 : (ri + 1) * 128]
                    sr, si = part[0:16], part[16:32]
                    vr = part[32:48] + slope * sr
                    vi = part[48:64] + slope * si
                    rows = (
                        (sr * tr - si * ti, sr * ti + si * tr),
                        (-(vr * ti + vi * tr), vr * tr - vi * ti),
                    )
                    for kind in range(2):
                        row = jnp.concatenate(rows[kind], axis=1)
                        hi = row.astype(BF16)
                        lo = (row - hi.astype(F32)).astype(BF16)
                        at = ((kind * ORD_ROW + o) * 2 + ri) * 16
                        lhs_ref[k, at : at + 16, :] = hi
                        lhs_ref[k, 1024 + at : 1024 + at + 16, :] = lo
    for k in range(3):
        y = jnp.dot(lhs_ref[k], w2_ref[k], preferred_element_type=F32)
        y = (y[1024:, :128] + y[:1024, 128:]) + y[:1024, :128]
        der_map, cos_map = ((0, 2), (1, 3), (4, 5))[k]
        for o in range(ORD_ROW):
            m = m_ref[order_slot(o, core)]
            pc, ps, sign = order_phase(m)
            factor = m.astype(F32) * (1.0 / LMAX)
            for ri in range(2):
                rows = pl.ds(o * 2 + ri, 16, stride=32)
                scale = -factor if ri == 0 else factor
                at = (o * 2 + 1 - ri) * 16
                os[cos_map, rows, :] = y[at : at + 16] * (half_sign(128, sign) * scale)
                at = ((ORD_ROW + o) * 2 + ri) * 16
                os[der_map, rows, :] = y[at : at + 16] * half_sign(128, -sign)
    for k in range(6):
        lanes = slice(k * 128, (k + 1) * 128)
        send_ref[:, lanes] = os[k, pl.ds((1 - core) * 256, 256), :].astype(BF16)
        keep_ref[:, lanes] = os[k, pl.ds(core * 256, 256), :].astype(BF16)


def pixel_kernel(*refs):
    x_refs, (f_ref, ft_ref, w_ref), out_refs = refs[:2], refs[2:5], refs[5:]
    low_in = lax.bitwise_and(lax.broadcasted_iota(jnp.int32, (1, 6 * 128), 1), 127) < 64
    low_out = lax.bitwise_and(lax.broadcasted_iota(jnp.int32, (1, 2 * 128), 1), 127) < 64

    def rows_of(i):
        chunks = [x_ref[i * 32 : i * 32 + 32, :] for x_ref in x_refs]
        return jnp.concatenate(chunks, axis=0).astype(F32)

    for pair in range(4):
        i0, i1 = 2 * pair, 2 * pair + 1
        x0, x1 = rows_of(i0), rows_of(i1)
        results = []
        for parity in range(2):
            if parity == 0:
                x = jnp.where(low_in, x0, x1)
            else:
                x = jnp.where(low_in, x1, x0)
            px = jnp.dot(ft_ref[parity], x.astype(BF16), preferred_element_type=F32)
            qt, ut, qp, up, dt, dp = (px[:, k * 128 : (k + 1) * 128] for k in range(6))
            deflected = jnp.concatenate([dt * qt + dp * qp, dt * ut + dp * up], axis=1)
            results.append(
                jnp.dot(f_ref[parity], deflected.astype(BF16), preferred_element_type=F32)
            )
        even, odd = results
        for i, g in ((i0, jnp.where(low_out, even, odd)), (i1, jnp.where(low_out, odd, even))):
            w = w_ref[i : i + 1, :]
            g = (g * jnp.concatenate([w, w], axis=1)).astype(BF16)
            for k in range(2):
                out_refs[k][i * 32 : i * 32 + 32, :] = g[k * 32 : k * 32 + 32]


def adjoint_kernel(m_ref, *refs):
    g_refs, (tw_ref, wadj_ref, w3_ref, out_ref, gs, os) = refs[:2], refs[2:]
    half, core = place()
    mine = pl.ds(half * 16, 16)
    for k in range(2):
        lanes = slice(k * 128, (k + 1) * 128)
        gs[k, pl.ds(core * 256, 256), :] = g_refs[0][:, lanes].astype(F32)
        gs[k, pl.ds((1 - core) * 256, 256), :] = g_refs[1][:, lanes].astype(F32)
    degree = degree_index()
    rows = []
    for o in range(ORD_ROW):
        pc, ps, sign = order_phase(m_ref[order_slot(o, core)])
        signs = half_sign(128, sign)
        for ri in range(2):
            rows += [gs[k, pl.ds(o * 2 + ri, 16, stride=32), :] * signs for k in range(2)]
    lhs = jnp.concatenate(rows, axis=0).astype(BF16)
    lhs = jnp.concatenate([lhs, lhs], axis=1)
    y = jnp.dot(lhs, wadj_ref[...], preferred_element_type=F32)
    for o in range(ORD_ROW):
        m = m_ref[order_slot(o, core)]
        inside = degree >= m
        pc, ps, sign = order_phase(m)
        turned = []
        for k in range(2):
            ar, ai = tw_ref[2 * k, mine, :], tw_ref[2 * k + 1, mine, :]
            turned.append((ar * pc + ai * ps, ai * pc - ar * ps))
        (pr, pi), (mr, mi) = turned
        for ri in range(2):
            at = (o * 2 + ri) * 32
            yq, yu = y[at : at + 16], y[at + 16 : at + 32]
            qr, qi, nr, ni = (yq[:, k * 128 : (k + 1) * 128] for k in range(4))
            ur, ui, vr, vi = (yu[:, k * 128 : (k + 1) * 128] for k in range(4))
            grad_re = pr * qr - pi * qi + mr * vr - mi * vi
            grad_im = pr * qi + pi * qr + mr * vi + mi * vr
            curl_re = pr * ur - pi * ui - mr * nr + mi * ni
            curl_im = pr * ui + pi * ur - mr * ni - mi * nr
            p = jnp.concatenate(
                [
                    jnp.concatenate([grad_re, curl_re], axis=1),
                    jnp.concatenate([grad_im, curl_im], axis=1),
                ],
                axis=0,
            )
            hi = p.astype(BF16)
            lo = (p - hi.astype(F32)).astype(BF16)
            rhs = jnp.concatenate([hi, lo, hi], axis=0)
            r = jnp.dot(w3_ref[half], rhs, preferred_element_type=F32)
            for part in range(2):
                value = jnp.where(inside, r[:, part * 128 : part * 128 + 128], 0.0)
                j = (o // 4) * 512 + (o % 4) * 4 + part * 2 + ri
                os[pl.ds(j, 32, stride=16), :] = value
    out_ref[...] = os[...].astype(BF16)


VMEM = pl.BlockSpec(memory_space=pltpu.VMEM)
SMEM = pl.BlockSpec(memory_space=pltpu.SMEM)
HBM = pl.BlockSpec(memory_space=pltpu.HBM)


def call(kernel, name, inputs, outs, scratch, spaces=None):
    specs = spaces or [SMEM if x.ndim == 1 else VMEM for x in inputs]
    single = len(outs) == 1
    out = pl.pallas_call(
        kernel,
        name=name,
        out_shape=[jax.ShapeDtypeStruct(s, d) for s, d in outs],
        in_specs=specs,
        out_specs=[SMEM if len(shape) == 1 else VMEM for shape, dtype in outs],
        scratch_shapes=scratch,
        compiler_params=pltpu.CompilerParams(vmem_limit_bytes=48 << 20),
    )(*inputs)
    return out[0] if single else out


def in_hbm(x):
    return pltpu.with_memory_space_constraint(x, pltpu.HBM)


def scratch(shape, dtype=F32):
    return pltpu.VMEM(shape, dtype)


def body(emode_coeffs, lensing_coeffs, order_values, circle_indices, circle_weights):
    const = {k: jnp.asarray(v) for k, v in CONST.items()}
    sent, orders = call(
        pack_kernel,
        "pack",
        [
            in_hbm(emode_coeffs.reshape(512, 128)),
            in_hbm(lensing_coeffs.reshape(512, 128)),
            in_hbm(order_values),
        ],
        [((2048, 128), BF16), ((32,), jnp.int32)],
        [
            scratch((2, 512, 128), BF16),
            scratch((2, 512, 128)),
            scratch((1024, 128)),
            pltpu.SemaphoreType.DMA((3,)),
        ],
        [HBM] * 3,
    )
    fourier, fourier_t, weights = call(
        table_kernel,
        "tables",
        [orders, circle_indices.reshape(32, 128), circle_weights.reshape(32, 128)],
        [((2, 64, LONGS), BF16), ((2, LONGS, 64), BF16), ((8, 128), F32)],
        [],
    )
    got = lax.all_to_all(sent.reshape(128, 16, 128), CHIPS, 0, 0, tiled=True)
    kept, passed = call(
        synth_kernel,
        "synth",
        [orders, got.reshape(2048, 128), const["w1"], const["tw"], const["w2"]],
        [((256, 768), BF16)] * 2,
        [scratch((2048, 128)), scratch((3, 2048, 256), BF16), scratch((6, 512, 128))],
    )
    held, handed = call(
        pixel_kernel,
        "pixel",
        [kept, swap_cores(passed), fourier, fourier_t, weights],
        [((256, 256), BF16)] * 2,
        [],
    )
    sums = call(
        adjoint_kernel,
        "adjoint",
        [orders, held, swap_cores(handed), const["tw"], const["wadj"], const["w3"]],
        [((2048, 128), BF16)],
        [scratch((2, 512, 128)), scratch((2048, 128))],
    )
    home = lax.all_to_all(sums.reshape(128, 16, 128), CHIPS, 0, 0, tiled=True)
    grad, curl = call(
        unpack_kernel,
        "unpack",
        [home.reshape(2048, 128)],
        [((512, 128), BF16), ((512, 128), BF16)],
        [scratch((1024, 128)), scratch((2, 512, 128))],
    )
    return grad.reshape(128, ORD_DEV, 128), curl.reshape(128, ORD_DEV, 128)


def solution(mesh):
    split = Mesh(mesh.devices.reshape(4, 2, 4, 4, 2), ALL)
    placed = P(("y", "x", "z"), ("row", "core"), None)
    return jax.shard_map(
        body,
        mesh=split,
        in_specs=(placed, placed, P(), P(), P()),
        out_specs=(placed, placed),
        check_vma=False,
    )
```

```python
import math

import jax
import jax.numpy as jnp
import numpy as np
from jax import lax
from jax.experimental import pallas as pl
from jax.experimental.pallas import tpu as pltpu
from jax.sharding import Mesh
from jax.sharding import PartitionSpec as P

LMAX = 4096
ORD_DEV = 4
ORD_ROW = 16
SIMS = 64
LONGS = 256
SPINS = (2, -2, 0)
ALL = ("row", "core", "y", "x", "z")


CHIPS = ("z", "row", "y", "x")


def place():
    return lax.axis_index("z"), lax.axis_index("core")


def order_slot(o, core):
    return (o // ORD_DEV) * 2 * ORD_DEV + core * ORD_DEV + o % ORD_DEV


def swap_cores(x):
    return lax.ppermute(x, "core", [(0, 1), (1, 0)])


F32 = jnp.float32
BF16 = jnp.bfloat16


def split_hi_lo(values):
    values = values.astype(np.float32)
    hi = values.astype(jnp.bfloat16)
    lo = (values - hi.astype(np.float32)).astype(jnp.bfloat16)
    return hi, lo


def make_constants():
    a = np.concatenate([np.arange(0, 32, 2), np.arange(1, 32, 2)])
    b = np.arange(128)
    c = np.arange(64)
    e = np.arange(32)
    amp = math.sqrt(2.0 / LMAX)
    first = np.pi * np.outer(2 * e + 1, a) / 64.0
    plain = np.concatenate([np.cos(first), np.sin(first)], axis=0)
    both = np.concatenate([plain, plain * (a / 32.0)[None, :]], axis=0)
    hi, lo = split_hi_lo(both)
    w1 = np.concatenate([hi, lo], axis=1).reshape(4, 2, 16, 64)
    w1 = w1.transpose(1, 0, 2, 3).reshape(2, 64, 64)
    twiddle, w2, wadj = [], [], []
    for s in SPINS:
        f = 2 * b + 1 + s
        t = np.pi * np.outer(2 * e + 1, f) / 16384.0
        twiddle += [amp * np.cos(t), amp * np.sin(t)]
        at_c = np.pi * np.outer(f, c) / 128.0
        at_n = np.pi * np.outer(f, c + 1) / 128.0
        full = np.concatenate(
            [
                np.concatenate([np.cos(at_c), np.cos(at_n)], axis=1),
                np.concatenate([-np.sin(at_c), np.sin(at_n)], axis=1),
            ],
            axis=0,
        )
        w2.append(np.concatenate(split_hi_lo(full), axis=1))
        if s:
            back = np.concatenate([full[:128].T, -full[128:].T], axis=1)
            wadj.append(np.concatenate(split_hi_lo(back), axis=0))
    last = np.stack([np.cos(first).T, -np.sin(first).T], axis=1).reshape(32, 2, 2, 16)
    hi, lo = split_hi_lo(last.transpose(2, 0, 1, 3).reshape(2, 32, 32))
    w3 = np.concatenate([hi, hi, lo], axis=2)
    return {
        "w1": w1,
        "tw": np.stack(twiddle).astype(np.float32),
        "w2": np.stack(w2),
        "wadj": np.concatenate(wadj, axis=1),
        "w3": w3,
    }


CONST = make_constants()


def order_phase(m):
    q = jnp.bitwise_and(m, 3)
    pc = jnp.where(q == 0, 1.0, jnp.where(q == 2, -1.0, 0.0)).astype(F32)
    ps = jnp.where(q == 1, 1.0, jnp.where(q == 3, -1.0, 0.0)).astype(F32)
    sign = jnp.where(jnp.bitwise_and(m, 1) == 0, 1.0, -1.0).astype(F32)
    return pc, ps, sign


def half_sign(width, value):
    lane = lax.broadcasted_iota(jnp.int32, (1, width), 1)
    return jnp.where(jnp.bitwise_and(lane, 127) < 64, jnp.float32(1.0), value)


def degree_index():
    row = lax.broadcasted_iota(jnp.int32, (32, 128), 0)
    a = jnp.bitwise_and(row, 15) * 2 + jnp.right_shift(row, 4)
    return a * 128 + lax.broadcasted_iota(jnp.int32, (32, 128), 1)


def chip_rows(o, j):
    at = (o // 4) * 256 + (o % 4) * 4 + j
    return [pl.ds(z * 1024 + at, 16, stride=16) for z in range(2)]


def fourier_tables(m_ref, core, f_ref, ft_ref):
    row = lax.broadcasted_iota(jnp.int32, (64, LONGS), 0)
    longitude = lax.broadcasted_iota(jnp.int32, (64, LONGS), 1)
    slot = jnp.right_shift(row, 1)
    m = jnp.zeros((64, LONGS), jnp.int32)
    for k in range(32):
        value = m_ref[order_slot(k % 16, core if k < 16 else 1 - core)]
        m = jnp.where(slot == k, value, m)
    quarter = jnp.bitwise_and(row, 1) * LMAX
    for parity in range(2):
        steps = jnp.bitwise_and(m * (2 * longitude + parity) + quarter, 4 * LMAX - 1)
        angles = steps.astype(F32) * (math.pi / (2 * LMAX))
        table = jnp.cos(angles) * (1.0 / math.sqrt(32))
        f_ref[parity] = table.astype(BF16)
        ft_ref[parity] = table.T.astype(BF16)


def weight_rows(row_pos, ci_ref, cw_ref, w_ref):
    e = lax.broadcasted_iota(jnp.int32, (16, 128), 0)
    ds = jnp.where(e < 8, row_pos * 8 + e, 71 - row_pos * 8 - e)
    cs = lax.broadcasted_iota(jnp.int32, (64, 128), 0)
    picked, chosen = [], []
    for k in range(32):
        circle = ci_ref[k : k + 1, :]
        low = jnp.bitwise_and(circle, 63)
        high = jnp.right_shift(circle, 6)
        chosen.append(jnp.where(high == cs, 1.0, 0.0).astype(BF16))
        w = jnp.where(low == ds, cw_ref[k : k + 1, :], 0.0)
        w_hi = w.astype(BF16)
        rest = w - w_hi.astype(F32)
        w_mid = rest.astype(BF16)
        w_lo = (rest - w_mid.astype(F32)).astype(BF16)
        picked.append(jnp.concatenate([w_hi, w_mid, w_lo], axis=0))
    w = lax.dot_general(
        jnp.concatenate(picked, axis=1),
        jnp.concatenate(chosen, axis=1),
        (((1,), (1,)), ((), ())),
        preferred_element_type=F32,
    )
    w = (w[32:] + w[16:32]) + w[:16]
    w_ref[...] = jnp.concatenate([w[:8], w[8:]], axis=1)


def table_kernel(m_ref, ci_ref, cw_ref, f_ref, ft_ref, w_ref):
    half, core = place()
    fourier_tables(m_ref, core, f_ref, ft_ref)
    weight_rows(2 * half + core, ci_ref, cw_ref, w_ref)


def pack_kernel(e_hbm, x_hbm, m_hbm, out_ref, m_ref, ex, src, dst, sems):
    copies = [
        pltpu.make_async_copy(e_hbm, ex.at[0], sems.at[0]),
        pltpu.make_async_copy(x_hbm, ex.at[1], sems.at[1]),
        pltpu.make_async_copy(m_hbm, m_ref, sems.at[2]),
    ]
    for copy in copies:
        copy.start()
    for field in range(2):
        copies[field].wait()
        src[field] = ex[field].astype(F32)
        for o in range(ORD_DEV):
            tile = src[field, pl.ds(o, 128, stride=ORD_DEV), :].T
            for ri in range(2):
                j = o * 4 + field * 2 + ri
                dst[pl.ds(j, 64, stride=16), :] = tile[ri * 64 : ri * 64 + 64, :]
    packed = dst[...].astype(BF16)
    out_ref[:1024] = packed
    out_ref[1024:] = packed
    copies[2].wait()


def unpack_kernel(in_ref, g_ref, c_ref, src, dst):
    src[...] = in_ref[:1024].astype(F32) + in_ref[1024:].astype(F32)
    for part, ref in enumerate((g_ref, c_ref)):
        for o in range(ORD_DEV):
            rows = []
            for ri in range(2):
                j = o * 4 + part * 2 + ri
                rows.append(src[pl.ds(j, 64, stride=16), :])
            dst[part, pl.ds(o, 128, stride=ORD_DEV), :] = jnp.concatenate(rows, axis=0).T
        ref[...] = dst[part].astype(BF16)


def synth_kernel(m_ref, x_ref, w1_ref, tw_ref, w2_ref, *refs):
    keep_ref, send_ref, xs, lhs_ref, os = refs
    half, core = place()
    mine = pl.ds(half * 16, 16)
    xs[...] = x_ref[...].astype(F32)
    degree = degree_index()
    lane = lax.broadcasted_iota(jnp.int32, (1, 128), 1)
    for o in range(ORD_ROW):
        m = m_ref[order_slot(o, core)]
        inside = degree >= m
        pc, ps, sign = order_phase(m)
        for field in range(2):
            tiles = []
            for ri in range(2):
                rows = chip_rows(o, field * 2 + ri)
                tile = jnp.concatenate([xs[at, :] for at in rows], axis=0)
                tiles.append(jnp.where(inside, tile, 0.0).astype(BF16))
            rhs = jnp.concatenate(tiles, axis=1)
            rhs = jnp.concatenate([rhs, rhs], axis=0)
            first = jnp.dot(w1_ref[half], rhs, preferred_element_type=F32)
            for k in (0, 1) if field == 0 else (2,):
                ar, ai = tw_ref[2 * k, mine, :], tw_ref[2 * k + 1, mine, :]
                tr = ar * pc + ai * ps
                ti = ai * pc - ar * ps
                slope = (2 * lane + 1 + SPINS[k]).astype(F32) * (1.0 / (2 * LMAX))
                for ri in range(2):
                    part = first[:, ri * 128 : (ri + 1) * 128]
                    sr, si = part[0:16], part[16:32]
                    vr = part[32:48] + slope * sr
                    vi = part[48:64] + slope * si
                    rows = (
                        (sr * tr - si * ti, sr * ti + si * tr),
                        (-(vr * ti + vi * tr), vr * tr - vi * ti),
                    )
                    for kind in range(2):
                        row = jnp.concatenate(rows[kind], axis=1)
                        hi = row.astype(BF16)
                        lo = (row - hi.astype(F32)).astype(BF16)
                        at = ((kind * ORD_ROW + o) * 2 + ri) * 16
                        lhs_ref[k, at : at + 16, :] = hi
                        lhs_ref[k, 1024 + at : 1024 + at + 16, :] = lo
    for k in range(3):
        y = jnp.dot(lhs_ref[k], w2_ref[k], preferred_element_type=F32)
        y = (y[1024:, :128] + y[:1024, 128:]) + y[:1024, :128]
        der_map, cos_map = ((0, 2), (1, 3), (4, 5))[k]
        for o in range(ORD_ROW):
            m = m_ref[order_slot(o, core)]
            pc, ps, sign = order_phase(m)
            factor = m.astype(F32) * (1.0 / LMAX)
            for ri in range(2):
                rows = pl.ds(o * 2 + ri, 16, stride=32)
                scale = -factor if ri == 0 else factor
                at = (o * 2 + 1 - ri) * 16
                os[cos_map, rows, :] = y[at : at + 16] * (half_sign(128, sign) * scale)
                at = ((ORD_ROW + o) * 2 + ri) * 16
                os[der_map, rows, :] = y[at : at + 16] * half_sign(128, -sign)
    for k in range(6):
        lanes = slice(k * 128, (k + 1) * 128)
        send_ref[:, lanes] = os[k, pl.ds((1 - core) * 256, 256), :].astype(BF16)
        keep_ref[:, lanes] = os[k, pl.ds(core * 256, 256), :].astype(BF16)


def pixel_kernel(*refs):
    x_refs, (f_ref, ft_ref, w_ref), out_refs = refs[:2], refs[2:5], refs[5:]
    low_in = lax.bitwise_and(lax.broadcasted_iota(jnp.int32, (1, 6 * 128), 1), 127) < 64
    low_out = lax.bitwise_and(lax.broadcasted_iota(jnp.int32, (1, 2 * 128), 1), 127) < 64

    def rows_of(i):
        chunks = [x_ref[i * 32 : i * 32 + 32, :] for x_ref in x_refs]
        return jnp.concatenate(chunks, axis=0).astype(F32)

    for pair in range(4):
        i0, i1 = 2 * pair, 2 * pair + 1
        x0, x1 = rows_of(i0), rows_of(i1)
        results = []
        for parity in range(2):
            if parity == 0:
                x = jnp.where(low_in, x0, x1)
            else:
                x = jnp.where(low_in, x1, x0)
            px = jnp.dot(ft_ref[parity], x.astype(BF16), preferred_element_type=F32)
            qt, ut, qp, up, dt, dp = (px[:, k * 128 : (k + 1) * 128] for k in range(6))
            deflected = jnp.concatenate([dt * qt + dp * qp, dt * ut + dp * up], axis=1)
            results.append(
                jnp.dot(f_ref[parity], deflected.astype(BF16), preferred_element_type=F32)
            )
        even, odd = results
        for i, g in ((i0, jnp.where(low_out, even, odd)), (i1, jnp.where(low_out, odd, even))):
            w = w_ref[i : i + 1, :]
            g = (g * jnp.concatenate([w, w], axis=1)).astype(BF16)
            for k in range(2):
                out_refs[k][i * 32 : i * 32 + 32, :] = g[k * 32 : k * 32 + 32]


def adjoint_kernel(m_ref, *refs):
    g_refs, (tw_ref, wadj_ref, w3_ref, out_ref, gs, os) = refs[:2], refs[2:]
    half, core = place()
    mine = pl.ds(half * 16, 16)
    for k in range(2):
        lanes = slice(k * 128, (k + 1) * 128)
        gs[k, pl.ds(core * 256, 256), :] = g_refs[0][:, lanes].astype(F32)
        gs[k, pl.ds((1 - core) * 256, 256), :] = g_refs[1][:, lanes].astype(F32)
    degree = degree_index()
    rows = []
    for o in range(ORD_ROW):
        pc, ps, sign = order_phase(m_ref[order_slot(o, core)])
        signs = half_sign(128, sign)
        for ri in range(2):
            rows += [gs[k, pl.ds(o * 2 + ri, 16, stride=32), :] * signs for k in range(2)]
    lhs = jnp.concatenate(rows, axis=0).astype(BF16)
    lhs = jnp.concatenate([lhs, lhs], axis=1)
    y = jnp.dot(lhs, wadj_ref[...], preferred_element_type=F32)
    for o in range(ORD_ROW):
        m = m_ref[order_slot(o, core)]
        inside = degree >= m
        pc, ps, sign = order_phase(m)
        turned = []
        for k in range(2):
            ar, ai = tw_ref[2 * k, mine, :], tw_ref[2 * k + 1, mine, :]
            turned.append((ar * pc + ai * ps, ai * pc - ar * ps))
        (pr, pi), (mr, mi) = turned
        for ri in range(2):
            at = (o * 2 + ri) * 32
            yq, yu = y[at : at + 16], y[at + 16 : at + 32]
            qr, qi, nr, ni = (yq[:, k * 128 : (k + 1) * 128] for k in range(4))
            ur, ui, vr, vi = (yu[:, k * 128 : (k + 1) * 128] for k in range(4))
            grad_re = pr * qr - pi * qi + mr * vr - mi * vi
            grad_im = pr * qi + pi * qr + mr * vi + mi * vr
            curl_re = pr * ur - pi * ui - mr * nr + mi * ni
            curl_im = pr * ui + pi * ur - mr * ni - mi * nr
            p = jnp.concatenate(
                [
                    jnp.concatenate([grad_re, curl_re], axis=1),
                    jnp.concatenate([grad_im, curl_im], axis=1),
                ],
                axis=0,
            )
            hi = p.astype(BF16)
            lo = (p - hi.astype(F32)).astype(BF16)
            rhs = jnp.concatenate([hi, lo, hi], axis=0)
            r = jnp.dot(w3_ref[half], rhs, preferred_element_type=F32)
            for part in range(2):
                value = jnp.where(inside, r[:, part * 128 : part * 128 + 128], 0.0)
                for z, at in enumerate(chip_rows(o, part * 2 + ri)):
                    os[at, :] = value[z * 16 : z * 16 + 16]
    out_ref[...] = os[...].astype(BF16)


VMEM = pl.BlockSpec(memory_space=pltpu.VMEM)
SMEM = pl.BlockSpec(memory_space=pltpu.SMEM)
HBM = pl.BlockSpec(memory_space=pltpu.HBM)


def call(kernel, name, inputs, outs, scratch, spaces=None):
    specs = spaces or [SMEM if x.ndim == 1 else VMEM for x in inputs]
    single = len(outs) == 1
    out = pl.pallas_call(
        kernel,
        name=name,
        out_shape=[jax.ShapeDtypeStruct(s, d) for s, d in outs],
        in_specs=specs,
        out_specs=[SMEM if len(shape) == 1 else VMEM for shape, dtype in outs],
        scratch_shapes=scratch,
        compiler_params=pltpu.CompilerParams(vmem_limit_bytes=48 << 20),
    )(*inputs)
    return out[0] if single else out


def in_hbm(x):
    return pltpu.with_memory_space_constraint(x, pltpu.HBM)


def scratch(shape, dtype=F32):
    return pltpu.VMEM(shape, dtype)


def body(emode_coeffs, lensing_coeffs, order_values, circle_indices, circle_weights):
    const = {k: jnp.asarray(v) for k, v in CONST.items()}
    sent, orders = call(
        pack_kernel,
        "pack",
        [
            in_hbm(emode_coeffs.reshape(512, 128)),
            in_hbm(lensing_coeffs.reshape(512, 128)),
            in_hbm(order_values),
        ],
        [((2048, 128), BF16), ((32,), jnp.int32)],
        [
            scratch((2, 512, 128), BF16),
            scratch((2, 512, 128)),
            scratch((1024, 128)),
            pltpu.SemaphoreType.DMA((3,)),
        ],
        [HBM] * 3,
    )
    fourier, fourier_t, weights = call(
        table_kernel,
        "tables",
        [orders, circle_indices.reshape(32, 128), circle_weights.reshape(32, 128)],
        [((2, 64, LONGS), BF16), ((2, LONGS, 64), BF16), ((8, 128), F32)],
        [],
    )
    got = lax.all_to_all(sent.reshape(128, 16, 128), CHIPS, 0, 0, tiled=True)
    kept, passed = call(
        synth_kernel,
        "synth",
        [orders, got.reshape(2048, 128), const["w1"], const["tw"], const["w2"]],
        [((256, 768), BF16)] * 2,
        [scratch((2048, 128)), scratch((3, 2048, 256), BF16), scratch((6, 512, 128))],
    )
    held, handed = call(
        pixel_kernel,
        "pixel",
        [kept, swap_cores(passed), fourier, fourier_t, weights],
        [((256, 256), BF16)] * 2,
        [],
    )
    sums = call(
        adjoint_kernel,
        "adjoint",
        [orders, held, swap_cores(handed), const["tw"], const["wadj"], const["w3"]],
        [((2048, 128), BF16)],
        [scratch((2, 512, 128)), scratch((2048, 128))],
    )
    home = lax.all_to_all(sums.reshape(128, 16, 128), CHIPS, 0, 0, tiled=True)
    grad, curl = call(
        unpack_kernel,
        "unpack",
        [home.reshape(2048, 128)],
        [((512, 128), BF16), ((512, 128), BF16)],
        [scratch((1024, 128)), scratch((2, 512, 128))],
    )
    return grad.reshape(128, ORD_DEV, 128), curl.reshape(128, ORD_DEV, 128)


def solution(mesh):
    split = Mesh(mesh.devices.reshape(4, 2, 4, 4, 2), ALL)
    placed = P(("y", "x", "z"), ("row", "core"), None)
    return jax.shard_map(
        body,
        mesh=split,
        in_specs=(placed, placed, P(), P(), P()),
        out_specs=(placed, placed),
        check_vma=False,
    )
```

```python
import math

import jax
import jax.numpy as jnp
import numpy as np
from jax import lax
from jax.experimental import pallas as pl
from jax.experimental.pallas import tpu as pltpu
from jax.sharding import Mesh
from jax.sharding import PartitionSpec as P

LMAX = 4096
ORD_DEV = 4
ORD_ROW = 16
SIMS = 64
LONGS = 256
SPINS = (2, -2, 0)
ALL = ("row", "core", "y", "x", "z")


CHIPS = ("z", "row", "y", "x")


def place():
    return lax.axis_index("z"), lax.axis_index("core")


def order_slot(o, core):
    return (o // ORD_DEV) * 2 * ORD_DEV + core * ORD_DEV + o % ORD_DEV


def swap_cores(x):
    return lax.ppermute(x, "core", [(0, 1), (1, 0)])


F32 = jnp.float32
BF16 = jnp.bfloat16


def split_hi_lo(values):
    values = values.astype(np.float32)
    hi = values.astype(jnp.bfloat16)
    lo = (values - hi.astype(np.float32)).astype(jnp.bfloat16)
    return hi, lo


def blocks(matrices, n):
    return np.stack([np.kron(np.eye(n, dtype=m.dtype), m) for m in matrices])


def make_constants():
    a = np.concatenate([np.arange(0, 32, 2), np.arange(1, 32, 2)])
    b = np.arange(128)
    c = np.arange(64)
    e = np.arange(32)
    amp = math.sqrt(2.0 / LMAX)
    first = np.pi * np.outer(2 * e + 1, a) / 64.0
    plain = np.concatenate([np.cos(first), np.sin(first)], axis=0)
    both = np.concatenate([plain, plain * (a / 32.0)[None, :]], axis=0)
    hi, lo = split_hi_lo(both)
    w1 = np.concatenate([hi, lo], axis=1).reshape(4, 2, 16, 64)
    w1 = blocks(w1.transpose(1, 0, 2, 3).reshape(2, 64, 64), 4)
    twiddle, w2, wadj = [], [], []
    for s in SPINS:
        f = 2 * b + 1 + s
        t = np.pi * np.outer(2 * e + 1, f) / 16384.0
        twiddle += [amp * np.cos(t), amp * np.sin(t)]
        at_c = np.pi * np.outer(f, c) / 128.0
        at_n = np.pi * np.outer(f, c + 1) / 128.0
        full = np.concatenate(
            [
                np.concatenate([np.cos(at_c), np.cos(at_n)], axis=1),
                np.concatenate([-np.sin(at_c), np.sin(at_n)], axis=1),
            ],
            axis=0,
        )
        w2.append(np.concatenate(split_hi_lo(full), axis=1))
        if s:
            back = np.concatenate([full[:128].T, -full[128:].T], axis=1)
            wadj.append(np.concatenate(split_hi_lo(back), axis=0))
    last = np.stack([np.cos(first).T, -np.sin(first).T], axis=1).reshape(32, 2, 2, 16)
    hi, lo = split_hi_lo(last.transpose(2, 0, 1, 3).reshape(2, 32, 32))
    w3 = blocks(np.concatenate([hi, hi, lo], axis=2), 2)
    return {
        "w1": w1,
        "tw": np.stack(twiddle).astype(np.float32),
        "w2": np.stack(w2),
        "wadj": np.concatenate(wadj, axis=1),
        "w3": w3,
    }


CONST = make_constants()


def order_phase(m):
    q = jnp.bitwise_and(m, 3)
    pc = jnp.where(q == 0, 1.0, jnp.where(q == 2, -1.0, 0.0)).astype(F32)
    ps = jnp.where(q == 1, 1.0, jnp.where(q == 3, -1.0, 0.0)).astype(F32)
    sign = jnp.where(jnp.bitwise_and(m, 1) == 0, 1.0, -1.0).astype(F32)
    return pc, ps, sign


def half_sign(width, value):
    lane = lax.broadcasted_iota(jnp.int32, (1, width), 1)
    return jnp.where(jnp.bitwise_and(lane, 127) < 64, jnp.float32(1.0), value)


def degree_index():
    row = lax.broadcasted_iota(jnp.int32, (32, 128), 0)
    a = jnp.bitwise_and(row, 15) * 2 + jnp.right_shift(row, 4)
    return a * 128 + lax.broadcasted_iota(jnp.int32, (32, 128), 1)


def chip_rows(o, j):
    at = (o // 4) * 256 + (o % 4) * 4 + j
    return [pl.ds(z * 1024 + at, 16, stride=16) for z in range(2)]


def fourier_tables(m_ref, core, f_ref, ft_ref):
    row = lax.broadcasted_iota(jnp.int32, (64, LONGS), 0)
    longitude = lax.broadcasted_iota(jnp.int32, (64, LONGS), 1)
    slot = jnp.right_shift(row, 1)
    m = jnp.zeros((64, LONGS), jnp.int32)
    for k in range(32):
        value = m_ref[order_slot(k % 16, core if k < 16 else 1 - core)]
        m = jnp.where(slot == k, value, m)
    quarter = jnp.bitwise_and(row, 1) * LMAX
    for parity in range(2):
        steps = jnp.bitwise_and(m * (2 * longitude + parity) + quarter, 4 * LMAX - 1)
        angles = steps.astype(F32) * (math.pi / (2 * LMAX))
        table = jnp.cos(angles) * (1.0 / math.sqrt(32))
        f_ref[parity] = table.astype(BF16)
        ft_ref[parity] = table.T.astype(BF16)


def weight_rows(row_pos, ci_ref, cw_ref, w_ref):
    e = lax.broadcasted_iota(jnp.int32, (16, 128), 0)
    ds = jnp.where(e < 8, row_pos * 8 + e, 71 - row_pos * 8 - e)
    cs = lax.broadcasted_iota(jnp.int32, (64, 128), 0)
    picked, chosen = [], []
    for k in range(32):
        circle = ci_ref[k : k + 1, :]
        low = jnp.bitwise_and(circle, 63)
        high = jnp.right_shift(circle, 6)
        chosen.append(jnp.where(high == cs, 1.0, 0.0).astype(BF16))
        w = jnp.where(low == ds, cw_ref[k : k + 1, :], 0.0)
        w_hi = w.astype(BF16)
        rest = w - w_hi.astype(F32)
        w_mid = rest.astype(BF16)
        w_lo = (rest - w_mid.astype(F32)).astype(BF16)
        picked.append(jnp.concatenate([w_hi, w_mid, w_lo], axis=0))
    w = lax.dot_general(
        jnp.concatenate(picked, axis=1),
        jnp.concatenate(chosen, axis=1),
        (((1,), (1,)), ((), ())),
        preferred_element_type=F32,
    )
    w = (w[32:] + w[16:32]) + w[:16]
    w_ref[...] = jnp.concatenate([w[:8], w[8:]], axis=1)


def table_kernel(m_ref, ci_ref, cw_ref, f_ref, ft_ref, w_ref):
    half, core = place()
    fourier_tables(m_ref, core, f_ref, ft_ref)
    weight_rows(2 * half + core, ci_ref, cw_ref, w_ref)


def pack_kernel(e_hbm, x_hbm, m_hbm, out_ref, m_ref, ex, src, dst, sems):
    copies = [
        pltpu.make_async_copy(e_hbm, ex.at[0], sems.at[0]),
        pltpu.make_async_copy(x_hbm, ex.at[1], sems.at[1]),
        pltpu.make_async_copy(m_hbm, m_ref, sems.at[2]),
    ]
    for copy in copies:
        copy.start()
    for field in range(2):
        copies[field].wait()
        src[field] = ex[field].astype(F32)
        for o in range(ORD_DEV):
            tile = src[field, pl.ds(o, 128, stride=ORD_DEV), :].T
            for ri in range(2):
                j = o * 4 + field * 2 + ri
                dst[pl.ds(j, 64, stride=16), :] = tile[ri * 64 : ri * 64 + 64, :]
    packed = dst[...].astype(BF16)
    out_ref[:1024] = packed
    out_ref[1024:] = packed
    copies[2].wait()


def unpack_kernel(in_ref, g_ref, c_ref, src, dst):
    src[...] = in_ref[:1024].astype(F32) + in_ref[1024:].astype(F32)
    for part, ref in enumerate((g_ref, c_ref)):
        for o in range(ORD_DEV):
            rows = []
            for ri in range(2):
                j = o * 4 + part * 2 + ri
                rows.append(src[pl.ds(j, 64, stride=16), :])
            dst[part, pl.ds(o, 128, stride=ORD_DEV), :] = jnp.concatenate(rows, axis=0).T
        ref[...] = dst[part].astype(BF16)


def synth_kernel(m_ref, x_ref, w1_ref, tw_ref, w2_ref, *refs):
    keep_ref, send_ref, xs, os = refs
    half, core = place()
    mine = pl.ds(half * 16, 16)
    xs[...] = x_ref[...].astype(F32)
    degree = degree_index()
    lane = lax.broadcasted_iota(jnp.int32, (1, 128), 1)
    for group in range(ORD_ROW // 4):
        first = []
        for field in range(2):
            tiles = []
            for o in range(group * 4, group * 4 + 4):
                inside = degree >= m_ref[order_slot(o, core)]
                pair = []
                for ri in range(2):
                    rows = chip_rows(o, field * 2 + ri)
                    tile = jnp.concatenate([xs[at, :] for at in rows], axis=0)
                    pair.append(jnp.where(inside, tile, 0.0).astype(BF16))
                tiles += [jnp.concatenate(pair, axis=1)] * 2
            rhs = jnp.concatenate(tiles, axis=0)
            first.append(jnp.dot(w1_ref[half], rhs, preferred_element_type=F32))
        phases = [order_phase(m_ref[order_slot(group * 4 + i, core)]) for i in range(4)]
        for k in (2, 0, 1):
            ar, ai = tw_ref[2 * k, mine, :], tw_ref[2 * k + 1, mine, :]
            slope = (2 * lane + 1 + SPINS[k]).astype(F32) * (1.0 / (2 * LMAX))
            rows = [[], []]
            for i in range(4):
                pc, ps, sign = phases[i]
                tr = ar * pc + ai * ps
                ti = ai * pc - ar * ps
                for ri in range(2):
                    part = first[k // 2][i * 64 : i * 64 + 64, ri * 128 : (ri + 1) * 128]
                    sr, si = part[0:16], part[16:32]
                    vr = part[32:48] + slope * sr
                    vi = part[48:64] + slope * si
                    rows[0].append(jnp.concatenate([sr * tr - si * ti, sr * ti + si * tr], axis=1))
                    rows[1].append(
                        jnp.concatenate([-(vr * ti + vi * tr), vr * tr - vi * ti], axis=1)
                    )
            row = jnp.concatenate(rows[0] + rows[1], axis=0)
            hi = row.astype(BF16)
            lo = (row - hi.astype(F32)).astype(BF16)
            y = jnp.dot(jnp.concatenate([hi, lo], axis=0), w2_ref[k], preferred_element_type=F32)
            y = (y[256:, :128] + y[:256, 128:]) + y[:256, :128]
            der_map, cos_map = ((0, 2), (1, 3), (4, 5))[k]
            for i in range(4):
                o = group * 4 + i
                sign = phases[i][2]
                factor = m_ref[order_slot(o, core)].astype(F32) * (1.0 / LMAX)
                for ri in range(2):
                    at = pl.ds(o * 2 + ri, 16, stride=32)
                    scale = -factor if ri == 0 else factor
                    c = (i * 2 + 1 - ri) * 16
                    d = 128 + (i * 2 + ri) * 16
                    os[cos_map, at, :] = y[c : c + 16] * (half_sign(128, sign) * scale)
                    os[der_map, at, :] = y[d : d + 16] * half_sign(128, -sign)
    for k in range(6):
        lanes = slice(k * 128, (k + 1) * 128)
        send_ref[:, lanes] = os[k, pl.ds((1 - core) * 256, 256), :].astype(BF16)
        keep_ref[:, lanes] = os[k, pl.ds(core * 256, 256), :].astype(BF16)


def pixel_kernel(*refs):
    x_refs, (f_ref, ft_ref, w_ref), out_refs = refs[:2], refs[2:5], refs[5:]
    low_in = lax.bitwise_and(lax.broadcasted_iota(jnp.int32, (1, 6 * 128), 1), 127) < 64
    low_out = lax.bitwise_and(lax.broadcasted_iota(jnp.int32, (1, 2 * 128), 1), 127) < 64

    def rows_of(i):
        chunks = [x_ref[i * 32 : i * 32 + 32, :] for x_ref in x_refs]
        return jnp.concatenate(chunks, axis=0)

    for pair in range(4):
        i0, i1 = 2 * pair, 2 * pair + 1
        x0, x1 = rows_of(i0), rows_of(i1)
        results = []
        for parity in range(2):
            if parity == 0:
                x = jnp.where(low_in, x0, x1)
            else:
                x = jnp.where(low_in, x1, x0)
            px = jnp.dot(ft_ref[parity], x, preferred_element_type=F32)
            qt, ut, qp, up, dt, dp = (px[:, k * 128 : (k + 1) * 128] for k in range(6))
            deflected = jnp.concatenate([dt * qt + dp * qp, dt * ut + dp * up], axis=1)
            results.append(
                jnp.dot(f_ref[parity], deflected.astype(BF16), preferred_element_type=F32)
            )
        even, odd = results
        for i, g in ((i0, jnp.where(low_out, even, odd)), (i1, jnp.where(low_out, odd, even))):
            w = w_ref[i : i + 1, :]
            g = (g * jnp.concatenate([w, w], axis=1)).astype(BF16)
            for k in range(2):
                out_refs[k][i * 32 : i * 32 + 32, :] = g[k * 32 : k * 32 + 32]


def adjoint_kernel(m_ref, *refs):
    g_refs, (tw_ref, wadj_ref, w3_ref, out_ref, gs, os) = refs[:2], refs[2:]
    half, core = place()
    mine = pl.ds(half * 16, 16)
    for k in range(2):
        lanes = slice(k * 128, (k + 1) * 128)
        gs[k, pl.ds(core * 256, 256), :] = g_refs[0][:, lanes].astype(F32)
        gs[k, pl.ds((1 - core) * 256, 256), :] = g_refs[1][:, lanes].astype(F32)
    degree = degree_index()
    rows = []
    for o in range(ORD_ROW):
        pc, ps, sign = order_phase(m_ref[order_slot(o, core)])
        signs = half_sign(128, sign)
        for ri in range(2):
            rows += [gs[k, pl.ds(o * 2 + ri, 16, stride=32), :] * signs for k in range(2)]
    lhs = jnp.concatenate(rows, axis=0).astype(BF16)
    lhs = jnp.concatenate([lhs, lhs], axis=1)
    y = jnp.dot(lhs, wadj_ref[...], preferred_element_type=F32)
    for o in range(ORD_ROW):
        m = m_ref[order_slot(o, core)]
        inside = degree >= m
        pc, ps, sign = order_phase(m)
        turned = []
        for k in range(2):
            ar, ai = tw_ref[2 * k, mine, :], tw_ref[2 * k + 1, mine, :]
            turned.append((ar * pc + ai * ps, ai * pc - ar * ps))
        (pr, pi), (mr, mi) = turned
        columns = []
        for ri in range(2):
            at = (o * 2 + ri) * 32
            yq, yu = y[at : at + 16], y[at + 16 : at + 32]
            qr, qi, nr, ni = (yq[:, k * 128 : (k + 1) * 128] for k in range(4))
            ur, ui, vr, vi = (yu[:, k * 128 : (k + 1) * 128] for k in range(4))
            grad_re = pr * qr - pi * qi + mr * vr - mi * vi
            grad_im = pr * qi + pi * qr + mr * vi + mi * vr
            curl_re = pr * ur - pi * ui - mr * nr + mi * ni
            curl_im = pr * ui + pi * ur - mr * ni - mi * nr
            p = jnp.concatenate(
                [
                    jnp.concatenate([grad_re, curl_re], axis=1),
                    jnp.concatenate([grad_im, curl_im], axis=1),
                ],
                axis=0,
            )
            hi = p.astype(BF16)
            lo = (p - hi.astype(F32)).astype(BF16)
            columns += [hi, lo, hi]
        rhs = jnp.concatenate(columns, axis=0)
        r = jnp.dot(w3_ref[half], rhs, preferred_element_type=F32)
        for ri in range(2):
            for part in range(2):
                value = r[ri * 32 : ri * 32 + 32, part * 128 : part * 128 + 128]
                value = jnp.where(inside, value, 0.0)
                for z, at in enumerate(chip_rows(o, part * 2 + ri)):
                    os[at, :] = value[z * 16 : z * 16 + 16]
    out_ref[...] = os[...].astype(BF16)


VMEM = pl.BlockSpec(memory_space=pltpu.VMEM)
SMEM = pl.BlockSpec(memory_space=pltpu.SMEM)
HBM = pl.BlockSpec(memory_space=pltpu.HBM)


def call(kernel, name, inputs, outs, scratch, spaces=None):
    specs = spaces or [SMEM if x.ndim == 1 else VMEM for x in inputs]
    single = len(outs) == 1
    out = pl.pallas_call(
        kernel,
        name=name,
        out_shape=[jax.ShapeDtypeStruct(s, d) for s, d in outs],
        in_specs=specs,
        out_specs=[VMEM for o in outs],
        scratch_shapes=scratch,
        compiler_params=pltpu.CompilerParams(vmem_limit_bytes=48 << 20),
    )(*inputs)
    return out[0] if single else out


def in_hbm(x):
    return pltpu.with_memory_space_constraint(x, pltpu.HBM)


def scratch(shape, dtype=F32):
    return pltpu.VMEM(shape, dtype)


def body(emode_coeffs, lensing_coeffs, order_values, circle_indices, circle_weights):
    const = {k: jnp.asarray(v) for k, v in CONST.items()}
    sent, orders = call(
        pack_kernel,
        "pack",
        [
            in_hbm(emode_coeffs.reshape(512, 128)),
            in_hbm(lensing_coeffs.reshape(512, 128)),
            in_hbm(order_values),
        ],
        [((2048, 128), BF16), ((32,), jnp.int32)],
        [
            scratch((2, 512, 128), BF16),
            scratch((2, 512, 128)),
            scratch((1024, 128)),
            pltpu.SemaphoreType.DMA((3,)),
        ],
        [HBM] * 3,
    )
    fourier, fourier_t, weights = call(
        table_kernel,
        "tables",
        [orders, circle_indices.reshape(32, 128), circle_weights.reshape(32, 128)],
        [((2, 64, LONGS), BF16), ((2, LONGS, 64), BF16), ((8, 128), F32)],
        [],
    )
    got = lax.all_to_all(sent.reshape(128, 16, 128), CHIPS, 0, 0, tiled=True)
    kept, passed = call(
        synth_kernel,
        "synth",
        [orders, got.reshape(2048, 128), const["w1"], const["tw"], const["w2"]],
        [((256, 768), BF16)] * 2,
        [scratch((2048, 128)), scratch((6, 512, 128))],
    )
    held, handed = call(
        pixel_kernel,
        "pixel",
        [kept, swap_cores(passed), fourier, fourier_t, weights],
        [((256, 256), BF16)] * 2,
        [],
    )
    sums = call(
        adjoint_kernel,
        "adjoint",
        [orders, held, swap_cores(handed), const["tw"], const["wadj"], const["w3"]],
        [((2048, 128), BF16)],
        [scratch((2, 512, 128)), scratch((2048, 128))],
    )
    home = lax.all_to_all(sums.reshape(128, 16, 128), CHIPS, 0, 0, tiled=True)
    grad, curl = call(
        unpack_kernel,
        "unpack",
        [home.reshape(2048, 128)],
        [((512, 128), BF16), ((512, 128), BF16)],
        [scratch((1024, 128)), scratch((2, 512, 128))],
    )
    return grad.reshape(128, ORD_DEV, 128), curl.reshape(128, ORD_DEV, 128)


def solution(mesh):
    split = Mesh(mesh.devices.reshape(4, 2, 4, 4, 2), ALL)
    placed = P(("y", "x", "z"), ("row", "core"), None)
    return jax.shard_map(
        body,
        mesh=split,
        in_specs=(placed, placed, P(), P(), P()),
        out_specs=(placed, placed),
        check_vma=False,
    )
```

```python
import math

import jax
import jax.numpy as jnp
import numpy as np
from jax import lax
from jax.experimental import pallas as pl
from jax.experimental.pallas import tpu as pltpu
from jax.sharding import Mesh
from jax.sharding import PartitionSpec as P

LMAX = 4096
ORD_DEV = 4
ORD_ROW = 16
SIMS = 64
LONGS = 256
SPINS = (2, -2, 0)
ALL = ("row", "core", "y", "x", "z")


CHIPS = ("z", "row", "y", "x")


def place():
    return lax.axis_index("z"), lax.axis_index("core")


def order_slot(o, core):
    return (o // ORD_DEV) * 2 * ORD_DEV + core * ORD_DEV + o % ORD_DEV


def swap_cores(x):
    return lax.ppermute(x, "core", [(0, 1), (1, 0)])


F32 = jnp.float32
BF16 = jnp.bfloat16


def split_hi_lo(values):
    values = values.astype(np.float32)
    hi = values.astype(jnp.bfloat16)
    lo = (values - hi.astype(np.float32)).astype(jnp.bfloat16)
    return hi, lo


def blocks(matrices, n):
    return np.stack([np.kron(np.eye(n, dtype=m.dtype), m) for m in matrices])


def make_constants():
    a = np.concatenate([np.arange(0, 32, 2), np.arange(1, 32, 2)])
    b = np.arange(128)
    c = np.arange(64)
    e = np.arange(32)
    amp = math.sqrt(2.0 / LMAX)
    first = np.pi * np.outer(2 * e + 1, a) / 64.0
    plain = np.concatenate([np.cos(first), np.sin(first)], axis=0)
    both = np.concatenate([plain, plain * (a / 32.0)[None, :]], axis=0)
    hi, lo = split_hi_lo(both)
    w1 = np.concatenate([hi, lo], axis=1).reshape(4, 2, 16, 64)
    w1 = blocks(w1.transpose(1, 0, 2, 3).reshape(2, 64, 64), 4)
    twiddle, w2, wadj = [], [], []
    for s in SPINS:
        f = 2 * b + 1 + s
        t = np.pi * np.outer(2 * e + 1, f) / 16384.0
        twiddle += [amp * np.cos(t), amp * np.sin(t)]
        at_c = np.pi * np.outer(f, c) / 128.0
        at_n = np.pi * np.outer(f, c + 1) / 128.0
        full = np.concatenate(
            [
                np.concatenate([np.cos(at_c), np.cos(at_n)], axis=1),
                np.concatenate([-np.sin(at_c), np.sin(at_n)], axis=1),
            ],
            axis=0,
        )
        w2.append(np.concatenate(split_hi_lo(full), axis=1))
        if s:
            back = np.concatenate([full[:128].T, -full[128:].T], axis=1)
            wadj.append(np.concatenate(split_hi_lo(back), axis=0))
    last = np.stack([np.cos(first).T, -np.sin(first).T], axis=1).reshape(32, 2, 2, 16)
    hi, lo = split_hi_lo(last.transpose(2, 0, 1, 3).reshape(2, 32, 32))
    w3 = blocks(np.concatenate([hi, hi, lo], axis=2), 2)
    return {
        "w1": w1,
        "tw": np.stack(twiddle).astype(np.float32),
        "w2": np.stack(w2),
        "wadj": np.concatenate(wadj, axis=1),
        "w3": w3,
    }


CONST = make_constants()


def order_phase(m):
    q = jnp.bitwise_and(m, 3)
    pc = jnp.where(q == 0, 1.0, jnp.where(q == 2, -1.0, 0.0)).astype(F32)
    ps = jnp.where(q == 1, 1.0, jnp.where(q == 3, -1.0, 0.0)).astype(F32)
    sign = jnp.where(jnp.bitwise_and(m, 1) == 0, 1.0, -1.0).astype(F32)
    return pc, ps, sign


def half_sign(width, value):
    lane = lax.broadcasted_iota(jnp.int32, (1, width), 1)
    return jnp.where(jnp.bitwise_and(lane, 127) < 64, jnp.float32(1.0), value)


def degree_index():
    row = lax.broadcasted_iota(jnp.int32, (32, 128), 0)
    a = jnp.bitwise_and(row, 15) * 2 + jnp.right_shift(row, 4)
    return a * 128 + lax.broadcasted_iota(jnp.int32, (32, 128), 1)


def chip_rows(o, j):
    at = (o // 4) * 256 + (o % 4) * 4 + j
    return [pl.ds(z * 1024 + at, 16, stride=16) for z in range(2)]


def fourier_tables(m_ref, core, f_ref, ft_ref):
    row = lax.broadcasted_iota(jnp.int32, (64, LONGS), 0)
    longitude = lax.broadcasted_iota(jnp.int32, (64, LONGS), 1)
    slot = jnp.right_shift(row, 1)
    m = jnp.zeros((64, LONGS), jnp.int32)
    for k in range(32):
        value = m_ref[order_slot(k % 16, core if k < 16 else 1 - core)]
        m = jnp.where(slot == k, value, m)
    quarter = jnp.bitwise_and(row, 1) * LMAX
    for parity in range(2):
        steps = jnp.bitwise_and(m * (2 * longitude + parity) + quarter, 4 * LMAX - 1)
        angles = steps.astype(F32) * (math.pi / (2 * LMAX))
        table = jnp.cos(angles) * (1.0 / math.sqrt(32))
        f_ref[parity] = table.astype(BF16)
        ft_ref[parity] = table.T.astype(BF16)


def weight_rows(row_pos, ci_ref, cw_ref, w_ref):
    e = lax.broadcasted_iota(jnp.int32, (16, 128), 0)
    ds = jnp.where(e < 8, row_pos * 8 + e, 71 - row_pos * 8 - e)
    cs = lax.broadcasted_iota(jnp.int32, (64, 128), 0)
    picked, chosen = [], []
    for k in range(32):
        circle = ci_ref[k : k + 1, :]
        low = jnp.bitwise_and(circle, 63)
        high = jnp.right_shift(circle, 6)
        chosen.append(jnp.where(high == cs, 1.0, 0.0).astype(BF16))
        w = jnp.where(low == ds, cw_ref[k : k + 1, :], 0.0)
        w_hi = w.astype(BF16)
        rest = w - w_hi.astype(F32)
        w_mid = rest.astype(BF16)
        w_lo = (rest - w_mid.astype(F32)).astype(BF16)
        picked.append(jnp.concatenate([w_hi, w_mid, w_lo], axis=0))
    w = lax.dot_general(
        jnp.concatenate(picked, axis=1),
        jnp.concatenate(chosen, axis=1),
        (((1,), (1,)), ((), ())),
        preferred_element_type=F32,
    )
    w = (w[32:] + w[16:32]) + w[:16]
    w_ref[...] = jnp.concatenate([w[:8], w[8:]], axis=1)


def table_kernel(m_ref, ci_ref, cw_ref, f_ref, ft_ref, w_ref):
    half, core = place()
    fourier_tables(m_ref, core, f_ref, ft_ref)
    weight_rows(2 * half + core, ci_ref, cw_ref, w_ref)


def pack_kernel(e_hbm, x_hbm, m_hbm, out_ref, m_ref, ex, src, dst, sems):
    copies = [
        pltpu.make_async_copy(e_hbm, ex.at[0], sems.at[0]),
        pltpu.make_async_copy(x_hbm, ex.at[1], sems.at[1]),
        pltpu.make_async_copy(m_hbm, m_ref, sems.at[2]),
    ]
    for copy in copies:
        copy.start()
    for field in range(2):
        copies[field].wait()
        src[field] = ex[field].astype(F32)
        for o in range(ORD_DEV):
            tile = src[field, pl.ds(o, 128, stride=ORD_DEV), :].T
            for ri in range(2):
                j = o * 4 + field * 2 + ri
                dst[pl.ds(j, 64, stride=16), :] = tile[ri * 64 : ri * 64 + 64, :]
    packed = dst[...].astype(BF16)
    out_ref[:1024] = packed
    out_ref[1024:] = packed
    copies[2].wait()


def unpack_kernel(in_ref, g_ref, c_ref, src, dst):
    src[...] = in_ref[:1024].astype(F32) + in_ref[1024:].astype(F32)
    for part, ref in enumerate((g_ref, c_ref)):
        for o in range(ORD_DEV):
            rows = []
            for ri in range(2):
                j = o * 4 + part * 2 + ri
                rows.append(src[pl.ds(j, 64, stride=16), :])
            dst[part, pl.ds(o, 128, stride=ORD_DEV), :] = jnp.concatenate(rows, axis=0).T
        ref[...] = dst[part].astype(BF16)


def synth_kernel(m_ref, x_ref, w1_ref, tw_ref, w2_ref, *refs):
    keep_ref, send_ref, xs, os = refs
    half, core = place()
    mine = pl.ds(half * 16, 16)
    xs[...] = x_ref[...].astype(F32)
    degree = degree_index()
    lane = lax.broadcasted_iota(jnp.int32, (1, 128), 1)
    for group in range(ORD_ROW // 4):
        first = []
        for field in range(2):
            tiles = []
            for o in range(group * 4, group * 4 + 4):
                inside = degree >= m_ref[order_slot(o, core)]
                pair = []
                for ri in range(2):
                    rows = chip_rows(o, field * 2 + ri)
                    tile = jnp.concatenate([xs[at, :] for at in rows], axis=0)
                    pair.append(jnp.where(inside, tile, 0.0).astype(BF16))
                tiles += [jnp.concatenate(pair, axis=1)] * 2
            rhs = jnp.concatenate(tiles, axis=0)
            first.append(jnp.dot(w1_ref[half], rhs, preferred_element_type=F32))
        phases = [order_phase(m_ref[order_slot(group * 4 + i, core)]) for i in range(4)]
        for k in (2, 0, 1):
            ar, ai = tw_ref[2 * k, mine, :], tw_ref[2 * k + 1, mine, :]
            slope = (2 * lane + 1 + SPINS[k]).astype(F32) * (1.0 / (2 * LMAX))
            rows = [[], []]
            for i in range(4):
                pc, ps, sign = phases[i]
                tr = ar * pc + ai * ps
                ti = ai * pc - ar * ps
                for ri in range(2):
                    part = first[k // 2][i * 64 : i * 64 + 64, ri * 128 : (ri + 1) * 128]
                    sr, si = part[0:16], part[16:32]
                    vr = part[32:48] + slope * sr
                    vi = part[48:64] + slope * si
                    rows[0].append(jnp.concatenate([sr * tr - si * ti, sr * ti + si * tr], axis=1))
                    rows[1].append(
                        jnp.concatenate([-(vr * ti + vi * tr), vr * tr - vi * ti], axis=1)
                    )
            row = jnp.concatenate(rows[0] + rows[1], axis=0)
            hi = row.astype(BF16)
            lo = (row - hi.astype(F32)).astype(BF16)
            y = jnp.dot(jnp.concatenate([hi, lo], axis=0), w2_ref[k], preferred_element_type=F32)
            y = (y[256:, :128] + y[:256, 128:]) + y[:256, :128]
            der_map, cos_map = ((0, 2), (1, 3), (4, 5))[k]
            for i in range(4):
                o = group * 4 + i
                sign = phases[i][2]
                factor = m_ref[order_slot(o, core)].astype(F32) * (1.0 / LMAX)
                for ri in range(2):
                    at = pl.ds(o * 2 + ri, 16, stride=32)
                    scale = -factor if ri == 0 else factor
                    c = (i * 2 + 1 - ri) * 16
                    d = 128 + (i * 2 + ri) * 16
                    os[cos_map, at, :] = y[c : c + 16] * (half_sign(128, sign) * scale)
                    os[der_map, at, :] = y[d : d + 16] * half_sign(128, -sign)
    for k in range(6):
        lanes = slice(k * 128, (k + 1) * 128)
        send_ref[:, lanes] = os[k, pl.ds((1 - core) * 256, 256), :].astype(BF16)
        keep_ref[:, lanes] = os[k, pl.ds(core * 256, 256), :].astype(BF16)


def pixel_kernel(*refs):
    x_refs, (f_ref, ft_ref, w_ref), out_refs = refs[:2], refs[2:5], refs[5:]
    low_in = lax.bitwise_and(lax.broadcasted_iota(jnp.int32, (1, 6 * 128), 1), 127) < 64
    low_out = lax.bitwise_and(lax.broadcasted_iota(jnp.int32, (1, 2 * 128), 1), 127) < 64

    def rows_of(i):
        chunks = [x_ref[i * 32 : i * 32 + 32, :] for x_ref in x_refs]
        return jnp.concatenate(chunks, axis=0)

    for pair in range(4):
        i0, i1 = 2 * pair, 2 * pair + 1
        x0, x1 = rows_of(i0), rows_of(i1)
        results = []
        for parity in range(2):
            if parity == 0:
                x = jnp.where(low_in, x0, x1)
            else:
                x = jnp.where(low_in, x1, x0)
            parts = []
            for at in range(0, LONGS, 64):
                ft = ft_ref[parity, at : at + 64, :]
                px = jnp.dot(ft, x, preferred_element_type=F32)
                qt, ut, qp, up, dt, dp = (px[:, k * 128 : (k + 1) * 128] for k in range(6))
                part = jnp.concatenate([dt * qt + dp * qp, dt * ut + dp * up], axis=1)
                parts.append(part.astype(BF16))
            deflected = jnp.concatenate(parts, axis=0)
            results.append(jnp.dot(f_ref[parity], deflected, preferred_element_type=F32))
        even, odd = results
        for i, g in ((i0, jnp.where(low_out, even, odd)), (i1, jnp.where(low_out, odd, even))):
            w = w_ref[i : i + 1, :]
            g = (g * jnp.concatenate([w, w], axis=1)).astype(BF16)
            for k in range(2):
                out_refs[k][i * 32 : i * 32 + 32, :] = g[k * 32 : k * 32 + 32]


def adjoint_kernel(m_ref, *refs):
    g_refs, (tw_ref, wadj_ref, w3_ref, out_ref, gs, os) = refs[:2], refs[2:]
    half, core = place()
    mine = pl.ds(half * 16, 16)
    for k in range(2):
        lanes = slice(k * 128, (k + 1) * 128)
        gs[k, pl.ds(core * 256, 256), :] = g_refs[0][:, lanes].astype(F32)
        gs[k, pl.ds((1 - core) * 256, 256), :] = g_refs[1][:, lanes].astype(F32)
    degree = degree_index()
    rows = []
    for o in range(ORD_ROW):
        pc, ps, sign = order_phase(m_ref[order_slot(o, core)])
        signs = half_sign(128, sign)
        for ri in range(2):
            rows += [gs[k, pl.ds(o * 2 + ri, 16, stride=32), :] * signs for k in range(2)]
    lhs = jnp.concatenate(rows, axis=0).astype(BF16)
    lhs = jnp.concatenate([lhs, lhs], axis=1)
    y = jnp.dot(lhs, wadj_ref[...], preferred_element_type=F32)
    for o in range(ORD_ROW):
        m = m_ref[order_slot(o, core)]
        inside = degree >= m
        pc, ps, sign = order_phase(m)
        turned = []
        for k in range(2):
            ar, ai = tw_ref[2 * k, mine, :], tw_ref[2 * k + 1, mine, :]
            turned.append((ar * pc + ai * ps, ai * pc - ar * ps))
        (pr, pi), (mr, mi) = turned
        columns = []
        for ri in range(2):
            at = (o * 2 + ri) * 32
            yq, yu = y[at : at + 16], y[at + 16 : at + 32]
            qr, qi, nr, ni = (yq[:, k * 128 : (k + 1) * 128] for k in range(4))
            ur, ui, vr, vi = (yu[:, k * 128 : (k + 1) * 128] for k in range(4))
            grad_re = pr * qr - pi * qi + mr * vr - mi * vi
            grad_im = pr * qi + pi * qr + mr * vi + mi * vr
            curl_re = pr * ur - pi * ui - mr * nr + mi * ni
            curl_im = pr * ui + pi * ur - mr * ni - mi * nr
            p = jnp.concatenate(
                [
                    jnp.concatenate([grad_re, curl_re], axis=1),
                    jnp.concatenate([grad_im, curl_im], axis=1),
                ],
                axis=0,
            )
            hi = p.astype(BF16)
            lo = (p - hi.astype(F32)).astype(BF16)
            columns += [hi, lo, hi]
        rhs = jnp.concatenate(columns, axis=0)
        r = jnp.dot(w3_ref[half], rhs, preferred_element_type=F32)
        for ri in range(2):
            for part in range(2):
                value = r[ri * 32 : ri * 32 + 32, part * 128 : part * 128 + 128]
                value = jnp.where(inside, value, 0.0)
                for z, at in enumerate(chip_rows(o, part * 2 + ri)):
                    os[at, :] = value[z * 16 : z * 16 + 16]
    out_ref[...] = os[...].astype(BF16)


VMEM = pl.BlockSpec(memory_space=pltpu.VMEM)
SMEM = pl.BlockSpec(memory_space=pltpu.SMEM)
HBM = pl.BlockSpec(memory_space=pltpu.HBM)


def call(kernel, name, inputs, outs, scratch, spaces=None):
    specs = spaces or [SMEM if x.ndim == 1 else VMEM for x in inputs]
    single = len(outs) == 1
    out = pl.pallas_call(
        kernel,
        name=name,
        out_shape=[jax.ShapeDtypeStruct(s, d) for s, d in outs],
        in_specs=specs,
        out_specs=[VMEM for o in outs],
        scratch_shapes=scratch,
        compiler_params=pltpu.CompilerParams(vmem_limit_bytes=48 << 20),
    )(*inputs)
    return out[0] if single else out


def in_hbm(x):
    return pltpu.with_memory_space_constraint(x, pltpu.HBM)


def scratch(shape, dtype=F32):
    return pltpu.VMEM(shape, dtype)


def body(emode_coeffs, lensing_coeffs, order_values, circle_indices, circle_weights):
    const = {k: jnp.asarray(v) for k, v in CONST.items()}
    sent, orders = call(
        pack_kernel,
        "pack",
        [
            in_hbm(emode_coeffs.reshape(512, 128)),
            in_hbm(lensing_coeffs.reshape(512, 128)),
            in_hbm(order_values),
        ],
        [((2048, 128), BF16), ((32,), jnp.int32)],
        [
            scratch((2, 512, 128), BF16),
            scratch((2, 512, 128)),
            scratch((1024, 128)),
            pltpu.SemaphoreType.DMA((3,)),
        ],
        [HBM] * 3,
    )
    fourier, fourier_t, weights = call(
        table_kernel,
        "tables",
        [orders, circle_indices.reshape(32, 128), circle_weights.reshape(32, 128)],
        [((2, 64, LONGS), BF16), ((2, LONGS, 64), BF16), ((8, 128), F32)],
        [],
    )
    got = lax.all_to_all(sent.reshape(128, 16, 128), CHIPS, 0, 0, tiled=True)
    kept, passed = call(
        synth_kernel,
        "synth",
        [orders, got.reshape(2048, 128), const["w1"], const["tw"], const["w2"]],
        [((256, 768), BF16)] * 2,
        [scratch((2048, 128)), scratch((6, 512, 128))],
    )
    held, handed = call(
        pixel_kernel,
        "pixel",
        [kept, swap_cores(passed), fourier, fourier_t, weights],
        [((256, 256), BF16)] * 2,
        [],
    )
    sums = call(
        adjoint_kernel,
        "adjoint",
        [orders, held, swap_cores(handed), const["tw"], const["wadj"], const["w3"]],
        [((2048, 128), BF16)],
        [scratch((2, 512, 128)), scratch((2048, 128))],
    )
    home = lax.all_to_all(sums.reshape(128, 16, 128), CHIPS, 0, 0, tiled=True)
    grad, curl = call(
        unpack_kernel,
        "unpack",
        [home.reshape(2048, 128)],
        [((512, 128), BF16), ((512, 128), BF16)],
        [scratch((1024, 128)), scratch((2, 512, 128))],
    )
    return grad.reshape(128, ORD_DEV, 128), curl.reshape(128, ORD_DEV, 128)


def solution(mesh):
    split = Mesh(mesh.devices.reshape(4, 2, 4, 4, 2), ALL)
    placed = P(("y", "x", "z"), ("row", "core"), None)
    return jax.shard_map(
        body,
        mesh=split,
        in_specs=(placed, placed, P(), P(), P()),
        out_specs=(placed, placed),
        check_vma=False,
    )
```

```python
import math

import jax
import jax.numpy as jnp
import numpy as np
from jax import lax
from jax.experimental import pallas as pl
from jax.experimental.pallas import tpu as pltpu
from jax.sharding import Mesh
from jax.sharding import PartitionSpec as P

LMAX = 4096
ORD_DEV = 4
ORD_ROW = 16
SIMS = 64
LONGS = 256
SPINS = (2, -2, 0)
ALL = ("row", "core", "y", "x", "z")


CHIPS = ("z", "row", "y", "x")


def place():
    return lax.axis_index("z"), lax.axis_index("core")


def order_slot(o, core):
    return (o // ORD_DEV) * 2 * ORD_DEV + core * ORD_DEV + o % ORD_DEV


def swap_cores(x):
    return lax.ppermute(x, "core", [(0, 1), (1, 0)])


F32 = jnp.float32
BF16 = jnp.bfloat16


def split_hi_lo(values):
    values = values.astype(np.float32)
    hi = values.astype(jnp.bfloat16)
    lo = (values - hi.astype(np.float32)).astype(jnp.bfloat16)
    return hi, lo


def blocks(matrices, n):
    return np.stack([np.kron(np.eye(n, dtype=m.dtype), m) for m in matrices])


def make_constants():
    a = np.concatenate([np.arange(0, 32, 2), np.arange(1, 32, 2)])
    b = np.arange(128)
    c = np.arange(64)
    e = np.arange(32)
    amp = math.sqrt(2.0 / LMAX)
    first = np.pi * np.outer(2 * e + 1, a) / 64.0
    plain = np.concatenate([np.cos(first), np.sin(first)], axis=0)
    both = np.concatenate([plain, plain * (a / 32.0)[None, :]], axis=0)
    hi, lo = split_hi_lo(both)
    w1 = np.concatenate([hi, lo], axis=1).reshape(4, 2, 16, 64)
    w1 = blocks(w1.transpose(1, 0, 2, 3).reshape(2, 64, 64), 4)
    twiddle, w2, wadj = [], [], []
    for s in SPINS:
        f = 2 * b + 1 + s
        t = np.pi * np.outer(2 * e + 1, f) / 16384.0
        twiddle += [amp * np.cos(t), amp * np.sin(t)]
        at_c = np.pi * np.outer(f, c) / 128.0
        at_n = np.pi * np.outer(f, c + 1) / 128.0
        full = np.concatenate(
            [
                np.concatenate([np.cos(at_c), np.cos(at_n)], axis=1),
                np.concatenate([-np.sin(at_c), np.sin(at_n)], axis=1),
            ],
            axis=0,
        )
        w2.append(np.concatenate(split_hi_lo(full), axis=1))
        if s:
            back = np.concatenate([full[:128].T, -full[128:].T], axis=1)
            wadj.append(np.concatenate(split_hi_lo(back), axis=0))
    last = np.stack([np.cos(first).T, -np.sin(first).T], axis=1).reshape(32, 2, 2, 16)
    hi, lo = split_hi_lo(last.transpose(2, 0, 1, 3).reshape(2, 32, 32))
    w3 = blocks(np.concatenate([hi, hi, lo], axis=2), 2)
    return {
        "w1": w1,
        "tw": np.stack(twiddle).astype(np.float32),
        "w2": np.stack(w2),
        "wadj": np.concatenate(wadj, axis=1),
        "w3": w3,
    }


CONST = make_constants()


def order_phase(m):
    q = jnp.bitwise_and(m, 3)
    pc = jnp.where(q == 0, 1.0, jnp.where(q == 2, -1.0, 0.0)).astype(F32)
    ps = jnp.where(q == 1, 1.0, jnp.where(q == 3, -1.0, 0.0)).astype(F32)
    sign = jnp.where(jnp.bitwise_and(m, 1) == 0, 1.0, -1.0).astype(F32)
    return pc, ps, sign


def half_sign(width, value):
    lane = lax.broadcasted_iota(jnp.int32, (1, width), 1)
    return jnp.where(jnp.bitwise_and(lane, 127) < 64, jnp.float32(1.0), value)


def degree_index():
    row = lax.broadcasted_iota(jnp.int32, (32, 128), 0)
    a = jnp.bitwise_and(row, 15) * 2 + jnp.right_shift(row, 4)
    return a * 128 + lax.broadcasted_iota(jnp.int32, (32, 128), 1)


def chip_rows(o, j):
    at = (o // 4) * 256 + (o % 4) * 4 + j
    return [pl.ds(z * 1024 + at, 16, stride=16) for z in range(2)]


def fourier_tables(m_ref, core, f_ref, ft_ref):
    row = lax.broadcasted_iota(jnp.int32, (64, LONGS), 0)
    longitude = lax.broadcasted_iota(jnp.int32, (64, LONGS), 1)
    slot = jnp.right_shift(row, 1)
    m = jnp.zeros((64, LONGS), jnp.int32)
    for k in range(32):
        value = m_ref[order_slot(k % 16, core if k < 16 else 1 - core)]
        m = jnp.where(slot == k, value, m)
    quarter = jnp.bitwise_and(row, 1) * LMAX
    for parity in range(2):
        steps = jnp.bitwise_and(m * (2 * longitude + parity) + quarter, 4 * LMAX - 1)
        angles = steps.astype(F32) * (math.pi / (2 * LMAX))
        table = jnp.cos(angles) * (1.0 / math.sqrt(32))
        f_ref[parity] = table.astype(BF16)
        ft_ref[parity] = table.T.astype(BF16)


def weight_rows(row_pos, ci_ref, cw_ref, w_ref):
    e = lax.broadcasted_iota(jnp.int32, (16, 128), 0)
    ds = jnp.where(e < 8, row_pos * 8 + e, 71 - row_pos * 8 - e)
    cs = lax.broadcasted_iota(jnp.int32, (64, 128), 0)
    picked, chosen = [], []
    for k in range(32):
        circle = ci_ref[k : k + 1, :]
        low = jnp.bitwise_and(circle, 63)
        high = jnp.right_shift(circle, 6)
        chosen.append(jnp.where(high == cs, 1.0, 0.0).astype(BF16))
        w = jnp.where(low == ds, cw_ref[k : k + 1, :], 0.0)
        w_hi = w.astype(BF16)
        rest = w - w_hi.astype(F32)
        w_mid = rest.astype(BF16)
        w_lo = (rest - w_mid.astype(F32)).astype(BF16)
        picked.append(jnp.concatenate([w_hi, w_mid, w_lo], axis=0))
    w = lax.dot_general(
        jnp.concatenate(picked, axis=1),
        jnp.concatenate(chosen, axis=1),
        (((1,), (1,)), ((), ())),
        preferred_element_type=F32,
    )
    w = (w[32:] + w[16:32]) + w[:16]
    w_ref[...] = jnp.concatenate([w[:8], w[8:]], axis=1)


def table_kernel(m_ref, ci_ref, cw_ref, f_ref, ft_ref, w_ref):
    half, core = place()
    fourier_tables(m_ref, core, f_ref, ft_ref)
    weight_rows(2 * half + core, ci_ref, cw_ref, w_ref)


def pack_kernel(e_hbm, x_hbm, m_hbm, out_ref, m_ref, ex, src, dst, sems):
    copies = [
        pltpu.make_async_copy(e_hbm, ex.at[0], sems.at[0]),
        pltpu.make_async_copy(x_hbm, ex.at[1], sems.at[1]),
        pltpu.make_async_copy(m_hbm, m_ref, sems.at[2]),
    ]
    for copy in copies:
        copy.start()
    for field in range(2):
        copies[field].wait()
        src[field] = ex[field].astype(F32)
        for o in range(ORD_DEV):
            tile = src[field, pl.ds(o, 128, stride=ORD_DEV), :].T
            for ri in range(2):
                j = o * 4 + field * 2 + ri
                dst[pl.ds(j, 64, stride=16), :] = tile[ri * 64 : ri * 64 + 64, :]
    packed = dst[...].astype(BF16)
    out_ref[:1024] = packed
    out_ref[1024:] = packed
    copies[2].wait()


def unpack_kernel(in_ref, g_ref, c_ref, src, dst):
    src[...] = in_ref[:1024].astype(F32) + in_ref[1024:].astype(F32)
    for part, ref in enumerate((g_ref, c_ref)):
        for o in range(ORD_DEV):
            rows = []
            for ri in range(2):
                j = o * 4 + part * 2 + ri
                rows.append(src[pl.ds(j, 64, stride=16), :])
            dst[part, pl.ds(o, 128, stride=ORD_DEV), :] = jnp.concatenate(rows, axis=0).T
        ref[...] = dst[part].astype(BF16)


def synth_kernel(m_ref, x_ref, w1_ref, tw_ref, w2_ref, *refs):
    keep_ref, send_ref, xs, os = refs
    half, core = place()
    mine = pl.ds(half * 16, 16)
    xs[...] = x_ref[...].astype(F32)
    degree = degree_index()
    lane = lax.broadcasted_iota(jnp.int32, (1, 128), 1)
    for group in range(ORD_ROW // 4):
        first = []
        for field in range(2):
            tiles = []
            for o in range(group * 4, group * 4 + 4):
                inside = degree >= m_ref[order_slot(o, core)]
                pair = []
                for ri in range(2):
                    rows = chip_rows(o, field * 2 + ri)
                    tile = jnp.concatenate([xs[at, :] for at in rows], axis=0)
                    pair.append(jnp.where(inside, tile, 0.0).astype(BF16))
                tiles += [jnp.concatenate(pair, axis=1)] * 2
            rhs = jnp.concatenate(tiles, axis=0)
            first.append(jnp.dot(w1_ref[half], rhs, preferred_element_type=F32))
        phases = [order_phase(m_ref[order_slot(group * 4 + i, core)]) for i in range(4)]
        for k in (2, 0, 1):
            ar, ai = tw_ref[2 * k, mine, :], tw_ref[2 * k + 1, mine, :]
            slope = (2 * lane + 1 + SPINS[k]).astype(F32) * (1.0 / (2 * LMAX))
            rows = [[], []]
            for i in range(4):
                pc, ps, sign = phases[i]
                tr = ar * pc + ai * ps
                ti = ai * pc - ar * ps
                for ri in range(2):
                    part = first[k // 2][i * 64 : i * 64 + 64, ri * 128 : (ri + 1) * 128]
                    sr, si = part[0:16], part[16:32]
                    vr = part[32:48] + slope * sr
                    vi = part[48:64] + slope * si
                    rows[0].append(jnp.concatenate([sr * tr - si * ti, sr * ti + si * tr], axis=1))
                    rows[1].append(
                        jnp.concatenate([-(vr * ti + vi * tr), vr * tr - vi * ti], axis=1)
                    )
            der_map, cos_map = ((0, 2), (1, 3), (4, 5))[k]
            for kind in range(2):
                row = jnp.concatenate(rows[kind], axis=0)
                hi = row.astype(BF16)
                lo = (row - hi.astype(F32)).astype(BF16)
                y = jnp.dot(
                    jnp.concatenate([hi, lo], axis=0), w2_ref[k], preferred_element_type=F32
                )
                y = (y[128:, :128] + y[:128, 128:]) + y[:128, :128]
                for i in range(4):
                    o = group * 4 + i
                    sign = phases[i][2]
                    factor = m_ref[order_slot(o, core)].astype(F32) * (1.0 / LMAX)
                    for ri in range(2):
                        at = pl.ds(o * 2 + ri, 16, stride=32)
                        if kind == 0:
                            scale = -factor if ri == 0 else factor
                            c = (i * 2 + 1 - ri) * 16
                            os[cos_map, at, :] = y[c : c + 16] * (half_sign(128, sign) * scale)
                        else:
                            d = (i * 2 + ri) * 16
                            os[der_map, at, :] = y[d : d + 16] * half_sign(128, -sign)
    for k in range(6):
        lanes = slice(k * 128, (k + 1) * 128)
        send_ref[:, lanes] = os[k, pl.ds((1 - core) * 256, 256), :].astype(BF16)
        keep_ref[:, lanes] = os[k, pl.ds(core * 256, 256), :].astype(BF16)


def pixel_kernel(*refs):
    x_refs, (f_ref, ft_ref, w_ref), out_refs = refs[:2], refs[2:5], refs[5:]
    low_in = lax.bitwise_and(lax.broadcasted_iota(jnp.int32, (1, 6 * 128), 1), 127) < 64
    low_out = lax.bitwise_and(lax.broadcasted_iota(jnp.int32, (1, 2 * 128), 1), 127) < 64

    def rows_of(i):
        chunks = [x_ref[i * 32 : i * 32 + 32, :] for x_ref in x_refs]
        return jnp.concatenate(chunks, axis=0)

    for pair in range(4):
        i0, i1 = 2 * pair, 2 * pair + 1
        x0, x1 = rows_of(i0), rows_of(i1)
        results = []
        for parity in range(2):
            if parity == 0:
                x = jnp.where(low_in, x0, x1)
            else:
                x = jnp.where(low_in, x1, x0)
            parts = []
            for at in range(0, LONGS, 64):
                ft = ft_ref[parity, at : at + 64, :]
                px = jnp.dot(ft, x, preferred_element_type=F32)
                qt, ut, qp, up, dt, dp = (px[:, k * 128 : (k + 1) * 128] for k in range(6))
                part = jnp.concatenate([dt * qt + dp * qp, dt * ut + dp * up], axis=1)
                parts.append(part.astype(BF16))
            deflected = jnp.concatenate(parts, axis=0)
            results.append(jnp.dot(f_ref[parity], deflected, preferred_element_type=F32))
        even, odd = results
        for i, g in ((i0, jnp.where(low_out, even, odd)), (i1, jnp.where(low_out, odd, even))):
            w = w_ref[i : i + 1, :]
            g = (g * jnp.concatenate([w, w], axis=1)).astype(BF16)
            for k in range(2):
                out_refs[k][i * 32 : i * 32 + 32, :] = g[k * 32 : k * 32 + 32]


def adjoint_kernel(m_ref, *refs):
    g_refs, (tw_ref, wadj_ref, w3_ref, out_ref, gs, os) = refs[:2], refs[2:]
    half, core = place()
    mine = pl.ds(half * 16, 16)
    for k in range(2):
        lanes = slice(k * 128, (k + 1) * 128)
        gs[k, pl.ds(core * 256, 256), :] = g_refs[0][:, lanes].astype(F32)
        gs[k, pl.ds((1 - core) * 256, 256), :] = g_refs[1][:, lanes].astype(F32)
    degree = degree_index()
    rows = []
    for o in range(ORD_ROW):
        pc, ps, sign = order_phase(m_ref[order_slot(o, core)])
        signs = half_sign(128, sign)
        for ri in range(2):
            rows += [gs[k, pl.ds(o * 2 + ri, 16, stride=32), :] * signs for k in range(2)]
    lhs = jnp.concatenate(rows, axis=0).astype(BF16)
    lhs = jnp.concatenate([lhs, lhs], axis=1)
    y = jnp.dot(lhs, wadj_ref[...], preferred_element_type=F32)
    for o in range(ORD_ROW):
        m = m_ref[order_slot(o, core)]
        inside = degree >= m
        pc, ps, sign = order_phase(m)
        turned = []
        for k in range(2):
            ar, ai = tw_ref[2 * k, mine, :], tw_ref[2 * k + 1, mine, :]
            turned.append((ar * pc + ai * ps, ai * pc - ar * ps))
        (pr, pi), (mr, mi) = turned
        columns = []
        for ri in range(2):
            at = (o * 2 + ri) * 32
            yq, yu = y[at : at + 16], y[at + 16 : at + 32]
            qr, qi, nr, ni = (yq[:, k * 128 : (k + 1) * 128] for k in range(4))
            ur, ui, vr, vi = (yu[:, k * 128 : (k + 1) * 128] for k in range(4))
            grad_re = pr * qr - pi * qi + mr * vr - mi * vi
            grad_im = pr * qi + pi * qr + mr * vi + mi * vr
            curl_re = pr * ur - pi * ui - mr * nr + mi * ni
            curl_im = pr * ui + pi * ur - mr * ni - mi * nr
            p = jnp.concatenate(
                [
                    jnp.concatenate([grad_re, curl_re], axis=1),
                    jnp.concatenate([grad_im, curl_im], axis=1),
                ],
                axis=0,
            )
            hi = p.astype(BF16)
            lo = (p - hi.astype(F32)).astype(BF16)
            columns += [hi, lo, hi]
        rhs = jnp.concatenate(columns, axis=0)
        r = jnp.dot(w3_ref[half], rhs, preferred_element_type=F32)
        for ri in range(2):
            for part in range(2):
                value = r[ri * 32 : ri * 32 + 32, part * 128 : part * 128 + 128]
                value = jnp.where(inside, value, 0.0)
                for z, at in enumerate(chip_rows(o, part * 2 + ri)):
                    os[at, :] = value[z * 16 : z * 16 + 16]
    out_ref[...] = os[...].astype(BF16)


VMEM = pl.BlockSpec(memory_space=pltpu.VMEM)
SMEM = pl.BlockSpec(memory_space=pltpu.SMEM)
HBM = pl.BlockSpec(memory_space=pltpu.HBM)


def call(kernel, name, inputs, outs, scratch, spaces=None):
    specs = spaces or [SMEM if x.ndim == 1 else VMEM for x in inputs]
    single = len(outs) == 1
    out = pl.pallas_call(
        kernel,
        name=name,
        out_shape=[jax.ShapeDtypeStruct(s, d) for s, d in outs],
        in_specs=specs,
        out_specs=[VMEM for o in outs],
        scratch_shapes=scratch,
        compiler_params=pltpu.CompilerParams(vmem_limit_bytes=48 << 20),
    )(*inputs)
    return out[0] if single else out


def in_hbm(x):
    return pltpu.with_memory_space_constraint(x, pltpu.HBM)


def scratch(shape, dtype=F32):
    return pltpu.VMEM(shape, dtype)


def body(emode_coeffs, lensing_coeffs, order_values, circle_indices, circle_weights):
    const = {k: jnp.asarray(v) for k, v in CONST.items()}
    sent, orders = call(
        pack_kernel,
        "pack",
        [
            in_hbm(emode_coeffs.reshape(512, 128)),
            in_hbm(lensing_coeffs.reshape(512, 128)),
            in_hbm(order_values),
        ],
        [((2048, 128), BF16), ((32,), jnp.int32)],
        [
            scratch((2, 512, 128), BF16),
            scratch((2, 512, 128)),
            scratch((1024, 128)),
            pltpu.SemaphoreType.DMA((3,)),
        ],
        [HBM] * 3,
    )
    fourier, fourier_t, weights = call(
        table_kernel,
        "tables",
        [orders, circle_indices.reshape(32, 128), circle_weights.reshape(32, 128)],
        [((2, 64, LONGS), BF16), ((2, LONGS, 64), BF16), ((8, 128), F32)],
        [],
    )
    got = lax.all_to_all(sent.reshape(128, 16, 128), CHIPS, 0, 0, tiled=True)
    kept, passed = call(
        synth_kernel,
        "synth",
        [orders, got.reshape(2048, 128), const["w1"], const["tw"], const["w2"]],
        [((256, 768), BF16)] * 2,
        [scratch((2048, 128)), scratch((6, 512, 128))],
    )
    held, handed = call(
        pixel_kernel,
        "pixel",
        [kept, swap_cores(passed), fourier, fourier_t, weights],
        [((256, 256), BF16)] * 2,
        [],
    )
    sums = call(
        adjoint_kernel,
        "adjoint",
        [orders, held, swap_cores(handed), const["tw"], const["wadj"], const["w3"]],
        [((2048, 128), BF16)],
        [scratch((2, 512, 128)), scratch((2048, 128))],
    )
    home = lax.all_to_all(sums.reshape(128, 16, 128), CHIPS, 0, 0, tiled=True)
    grad, curl = call(
        unpack_kernel,
        "unpack",
        [home.reshape(2048, 128)],
        [((512, 128), BF16), ((512, 128), BF16)],
        [scratch((1024, 128)), scratch((2, 512, 128))],
    )
    return grad.reshape(128, ORD_DEV, 128), curl.reshape(128, ORD_DEV, 128)


def solution(mesh):
    split = Mesh(mesh.devices.reshape(4, 2, 4, 4, 2), ALL)
    placed = P(("y", "x", "z"), ("row", "core"), None)
    return jax.shard_map(
        body,
        mesh=split,
        in_specs=(placed, placed, P(), P(), P()),
        out_specs=(placed, placed),
        check_vma=False,
    )
```

```python
import math

import jax
import jax.numpy as jnp
import numpy as np
from jax import lax
from jax.experimental import pallas as pl
from jax.experimental.pallas import tpu as pltpu
from jax.sharding import Mesh
from jax.sharding import PartitionSpec as P

LMAX = 4096
ORD_DEV = 4
ORD_ROW = 16
SIMS = 64
LONGS = 256
SPINS = (2, -2, 0)
ALL = ("row", "core", "y", "x", "z")


CHIPS = ("z", "row", "y", "x")


def place():
    return lax.axis_index("z"), lax.axis_index("core")


def order_slot(o, core):
    return (o // ORD_DEV) * 2 * ORD_DEV + core * ORD_DEV + o % ORD_DEV


def swap_cores(x):
    return lax.ppermute(x, "core", [(0, 1), (1, 0)])


F32 = jnp.float32
BF16 = jnp.bfloat16


def split_hi_lo(values):
    values = values.astype(np.float32)
    hi = values.astype(jnp.bfloat16)
    lo = (values - hi.astype(np.float32)).astype(jnp.bfloat16)
    return hi, lo


def blocks(matrices, n):
    return np.stack([np.kron(np.eye(n, dtype=m.dtype), m) for m in matrices])


def make_constants():
    a = np.concatenate([np.arange(0, 32, 2), np.arange(1, 32, 2)])
    b = np.arange(128)
    c = np.arange(64)
    e = np.arange(32)
    amp = math.sqrt(2.0 / LMAX)
    first = np.pi * np.outer(2 * e + 1, a) / 64.0
    plain = np.concatenate([np.cos(first), np.sin(first)], axis=0)
    both = np.concatenate([plain, plain * (a / 32.0)[None, :]], axis=0)
    hi, lo = split_hi_lo(both)
    w1 = np.concatenate([hi, lo], axis=1).reshape(4, 2, 16, 64)
    w1 = blocks(w1.transpose(1, 0, 2, 3).reshape(2, 64, 64), 4)
    twiddle, w2, wadj = [], [], []
    for s in SPINS:
        f = 2 * b + 1 + s
        t = np.pi * np.outer(2 * e + 1, f) / 16384.0
        twiddle += [amp * np.cos(t), amp * np.sin(t)]
        at_c = np.pi * np.outer(f, c) / 128.0
        at_n = np.pi * np.outer(f, c + 1) / 128.0
        full = np.concatenate(
            [
                np.concatenate([np.cos(at_c), np.cos(at_n)], axis=1),
                np.concatenate([-np.sin(at_c), np.sin(at_n)], axis=1),
            ],
            axis=0,
        )
        w2.append(np.concatenate(split_hi_lo(full), axis=1))
        if s:
            back = np.concatenate([full[:128].T, -full[128:].T], axis=1)
            wadj.append(np.concatenate(split_hi_lo(back), axis=0))
    last = np.stack([np.cos(first).T, -np.sin(first).T], axis=1).reshape(32, 2, 2, 16)
    hi, lo = split_hi_lo(last.transpose(2, 0, 1, 3).reshape(2, 32, 32))
    w3 = blocks(np.concatenate([hi, hi, lo], axis=2), 2)
    return {
        "w1": w1,
        "tw": np.stack(twiddle).astype(np.float32),
        "w2": np.stack(w2),
        "wadj": np.concatenate(wadj, axis=1),
        "w3": w3,
    }


CONST = make_constants()


def order_phase(m):
    q = jnp.bitwise_and(m, 3)
    pc = jnp.where(q == 0, 1.0, jnp.where(q == 2, -1.0, 0.0)).astype(F32)
    ps = jnp.where(q == 1, 1.0, jnp.where(q == 3, -1.0, 0.0)).astype(F32)
    sign = jnp.where(jnp.bitwise_and(m, 1) == 0, 1.0, -1.0).astype(F32)
    return pc, ps, sign


def half_sign(width, value):
    lane = lax.broadcasted_iota(jnp.int32, (1, width), 1)
    return jnp.where(jnp.bitwise_and(lane, 127) < 64, jnp.float32(1.0), value)


def degree_index():
    row = lax.broadcasted_iota(jnp.int32, (32, 128), 0)
    a = jnp.bitwise_and(row, 15) * 2 + jnp.right_shift(row, 4)
    return a * 128 + lax.broadcasted_iota(jnp.int32, (32, 128), 1)


def chip_rows(o, j):
    at = (o // 4) * 256 + (o % 4) * 4 + j
    return [pl.ds(z * 1024 + at, 16, stride=16) for z in range(2)]


def fourier_tables(m_ref, core, f_ref, ft_ref):
    row = lax.broadcasted_iota(jnp.int32, (64, LONGS), 0)
    longitude = lax.broadcasted_iota(jnp.int32, (64, LONGS), 1)
    slot = jnp.right_shift(row, 1)
    m = jnp.zeros((64, LONGS), jnp.int32)
    for k in range(32):
        value = m_ref[order_slot(k % 16, core if k < 16 else 1 - core)]
        m = jnp.where(slot == k, value, m)
    quarter = jnp.bitwise_and(row, 1) * LMAX
    for parity in range(2):
        steps = jnp.bitwise_and(m * (2 * longitude + parity) + quarter, 4 * LMAX - 1)
        angles = steps.astype(F32) * (math.pi / (2 * LMAX))
        table = jnp.cos(angles) * (1.0 / math.sqrt(32))
        f_ref[parity] = table.astype(BF16)
        ft_ref[parity] = table.T.astype(BF16)


def weight_rows(row_pos, ci_ref, cw_ref, w_ref):
    e = lax.broadcasted_iota(jnp.int32, (16, 128), 0)
    ds = jnp.where(e < 8, row_pos * 8 + e, 71 - row_pos * 8 - e)
    cs = lax.broadcasted_iota(jnp.int32, (64, 128), 0)
    picked, chosen = [], []
    for k in range(32):
        circle = ci_ref[k : k + 1, :]
        low = jnp.bitwise_and(circle, 63)
        high = jnp.right_shift(circle, 6)
        chosen.append(jnp.where(high == cs, 1.0, 0.0).astype(BF16))
        w = jnp.where(low == ds, cw_ref[k : k + 1, :], 0.0)
        w_hi = w.astype(BF16)
        rest = w - w_hi.astype(F32)
        w_mid = rest.astype(BF16)
        w_lo = (rest - w_mid.astype(F32)).astype(BF16)
        picked.append(jnp.concatenate([w_hi, w_mid, w_lo], axis=0))
    w = lax.dot_general(
        jnp.concatenate(picked, axis=1),
        jnp.concatenate(chosen, axis=1),
        (((1,), (1,)), ((), ())),
        preferred_element_type=F32,
    )
    w = (w[32:] + w[16:32]) + w[:16]
    w_ref[...] = jnp.concatenate([w[:8], w[8:]], axis=1)


def table_kernel(m_ref, ci_ref, cw_ref, f_ref, ft_ref, w_ref):
    half, core = place()
    fourier_tables(m_ref, core, f_ref, ft_ref)
    weight_rows(2 * half + core, ci_ref, cw_ref, w_ref)


def pack_kernel(e_hbm, x_hbm, m_hbm, out_ref, m_ref, ex, src, dst, sems):
    copies = [
        pltpu.make_async_copy(e_hbm, ex.at[0], sems.at[0]),
        pltpu.make_async_copy(x_hbm, ex.at[1], sems.at[1]),
        pltpu.make_async_copy(m_hbm, m_ref, sems.at[2]),
    ]
    for copy in copies:
        copy.start()
    for field in range(2):
        copies[field].wait()
        src[field] = ex[field].astype(F32)
        for o in range(ORD_DEV):
            tile = src[field, pl.ds(o, 128, stride=ORD_DEV), :].T
            for ri in range(2):
                j = o * 4 + field * 2 + ri
                dst[pl.ds(j, 64, stride=16), :] = tile[ri * 64 : ri * 64 + 64, :]
    packed = dst[...].astype(BF16)
    out_ref[:1024] = packed
    out_ref[1024:] = packed
    copies[2].wait()


def unpack_kernel(in_ref, g_hbm, c_hbm, src, dst, out, sems):
    src[...] = in_ref[:1024].astype(F32) + in_ref[1024:].astype(F32)
    copies = []
    for part, hbm in enumerate((g_hbm, c_hbm)):
        for o in range(ORD_DEV):
            rows = []
            for ri in range(2):
                j = o * 4 + part * 2 + ri
                rows.append(src[pl.ds(j, 64, stride=16), :])
            dst[part, pl.ds(o, 128, stride=ORD_DEV), :] = jnp.concatenate(rows, axis=0).T
        out[part] = dst[part].astype(BF16)
        copies.append(pltpu.make_async_copy(out.at[part], hbm, sems.at[part]))
        copies[part].start()
    for copy in copies:
        copy.wait()


def synth_kernel(m_ref, x_ref, w1_ref, tw_ref, w2_ref, *refs):
    keep_ref, send_ref, xs, os = refs
    half, core = place()
    mine = pl.ds(half * 16, 16)
    xs[...] = x_ref[...].astype(F32)
    degree = degree_index()
    lane = lax.broadcasted_iota(jnp.int32, (1, 128), 1)
    for group in range(ORD_ROW // 4):
        first = []
        for field in range(2):
            tiles = []
            for o in range(group * 4, group * 4 + 4):
                inside = degree >= m_ref[order_slot(o, core)]
                pair = []
                for ri in range(2):
                    rows = chip_rows(o, field * 2 + ri)
                    tile = jnp.concatenate([xs[at, :] for at in rows], axis=0)
                    pair.append(jnp.where(inside, tile, 0.0).astype(BF16))
                tiles += [jnp.concatenate(pair, axis=1)] * 2
            rhs = jnp.concatenate(tiles, axis=0)
            first.append(jnp.dot(w1_ref[half], rhs, preferred_element_type=F32))
        phases = [order_phase(m_ref[order_slot(group * 4 + i, core)]) for i in range(4)]
        for k in (2, 0, 1):
            ar, ai = tw_ref[2 * k, mine, :], tw_ref[2 * k + 1, mine, :]
            slope = (2 * lane + 1 + SPINS[k]).astype(F32) * (1.0 / (2 * LMAX))
            rows = [[], []]
            for i in range(4):
                pc, ps, sign = phases[i]
                tr = ar * pc + ai * ps
                ti = ai * pc - ar * ps
                for ri in range(2):
                    part = first[k // 2][i * 64 : i * 64 + 64, ri * 128 : (ri + 1) * 128]
                    sr, si = part[0:16], part[16:32]
                    vr = part[32:48] + slope * sr
                    vi = part[48:64] + slope * si
                    rows[0].append(jnp.concatenate([sr * tr - si * ti, sr * ti + si * tr], axis=1))
                    rows[1].append(
                        jnp.concatenate([-(vr * ti + vi * tr), vr * tr - vi * ti], axis=1)
                    )
            der_map, cos_map = ((0, 2), (1, 3), (4, 5))[k]
            for kind in range(2):
                row = jnp.concatenate(rows[kind], axis=0)
                hi = row.astype(BF16)
                lo = (row - hi.astype(F32)).astype(BF16)
                y = jnp.dot(
                    jnp.concatenate([hi, lo], axis=0), w2_ref[k], preferred_element_type=F32
                )
                y = (y[128:, :128] + y[:128, 128:]) + y[:128, :128]
                for i in range(4):
                    o = group * 4 + i
                    sign = phases[i][2]
                    factor = m_ref[order_slot(o, core)].astype(F32) * (1.0 / LMAX)
                    for ri in range(2):
                        at = pl.ds(o * 2 + ri, 16, stride=32)
                        if kind == 0:
                            scale = -factor if ri == 0 else factor
                            c = (i * 2 + 1 - ri) * 16
                            os[cos_map, at, :] = y[c : c + 16] * (half_sign(128, sign) * scale)
                        else:
                            d = (i * 2 + ri) * 16
                            os[der_map, at, :] = y[d : d + 16] * half_sign(128, -sign)
    for k in range(6):
        lanes = slice(k * 128, (k + 1) * 128)
        send_ref[:, lanes] = os[k, pl.ds((1 - core) * 256, 256), :].astype(BF16)
        keep_ref[:, lanes] = os[k, pl.ds(core * 256, 256), :].astype(BF16)


def pixel_kernel(*refs):
    x_refs, (f_ref, ft_ref, w_ref), out_refs = refs[:2], refs[2:5], refs[5:]
    low_in = lax.bitwise_and(lax.broadcasted_iota(jnp.int32, (1, 6 * 128), 1), 127) < 64
    low_out = lax.bitwise_and(lax.broadcasted_iota(jnp.int32, (1, 2 * 128), 1), 127) < 64

    def rows_of(i):
        chunks = [x_ref[i * 32 : i * 32 + 32, :] for x_ref in x_refs]
        return jnp.concatenate(chunks, axis=0)

    for pair in range(4):
        i0, i1 = 2 * pair, 2 * pair + 1
        x0, x1 = rows_of(i0), rows_of(i1)
        results = []
        for parity in range(2):
            if parity == 0:
                x = jnp.where(low_in, x0, x1)
            else:
                x = jnp.where(low_in, x1, x0)
            parts = []
            for at in range(0, LONGS, 64):
                ft = ft_ref[parity, at : at + 64, :]
                px = jnp.dot(ft, x, preferred_element_type=F32)
                qt, ut, qp, up, dt, dp = (px[:, k * 128 : (k + 1) * 128] for k in range(6))
                part = jnp.concatenate([dt * qt + dp * qp, dt * ut + dp * up], axis=1)
                parts.append(part.astype(BF16))
            deflected = jnp.concatenate(parts, axis=0)
            results.append(jnp.dot(f_ref[parity], deflected, preferred_element_type=F32))
        even, odd = results
        for i, g in ((i0, jnp.where(low_out, even, odd)), (i1, jnp.where(low_out, odd, even))):
            w = w_ref[i : i + 1, :]
            g = (g * jnp.concatenate([w, w], axis=1)).astype(BF16)
            for k in range(2):
                out_refs[k][i * 32 : i * 32 + 32, :] = g[k * 32 : k * 32 + 32]


def adjoint_kernel(m_ref, *refs):
    g_refs, (tw_ref, wadj_ref, w3_ref, out_ref, gs, os) = refs[:2], refs[2:]
    half, core = place()
    mine = pl.ds(half * 16, 16)
    for k in range(2):
        lanes = slice(k * 128, (k + 1) * 128)
        gs[k, pl.ds(core * 256, 256), :] = g_refs[0][:, lanes].astype(F32)
        gs[k, pl.ds((1 - core) * 256, 256), :] = g_refs[1][:, lanes].astype(F32)
    degree = degree_index()
    rows = []
    for o in range(ORD_ROW):
        pc, ps, sign = order_phase(m_ref[order_slot(o, core)])
        signs = half_sign(128, sign)
        for ri in range(2):
            rows += [gs[k, pl.ds(o * 2 + ri, 16, stride=32), :] * signs for k in range(2)]
    lhs = jnp.concatenate(rows, axis=0).astype(BF16)
    lhs = jnp.concatenate([lhs, lhs], axis=1)
    y = jnp.dot(lhs, wadj_ref[...], preferred_element_type=F32)
    for o in range(ORD_ROW):
        m = m_ref[order_slot(o, core)]
        inside = degree >= m
        pc, ps, sign = order_phase(m)
        turned = []
        for k in range(2):
            ar, ai = tw_ref[2 * k, mine, :], tw_ref[2 * k + 1, mine, :]
            turned.append((ar * pc + ai * ps, ai * pc - ar * ps))
        (pr, pi), (mr, mi) = turned
        columns = []
        for ri in range(2):
            at = (o * 2 + ri) * 32
            yq, yu = y[at : at + 16], y[at + 16 : at + 32]
            qr, qi, nr, ni = (yq[:, k * 128 : (k + 1) * 128] for k in range(4))
            ur, ui, vr, vi = (yu[:, k * 128 : (k + 1) * 128] for k in range(4))
            grad_re = pr * qr - pi * qi + mr * vr - mi * vi
            grad_im = pr * qi + pi * qr + mr * vi + mi * vr
            curl_re = pr * ur - pi * ui - mr * nr + mi * ni
            curl_im = pr * ui + pi * ur - mr * ni - mi * nr
            p = jnp.concatenate(
                [
                    jnp.concatenate([grad_re, curl_re], axis=1),
                    jnp.concatenate([grad_im, curl_im], axis=1),
                ],
                axis=0,
            )
            hi = p.astype(BF16)
            lo = (p - hi.astype(F32)).astype(BF16)
            columns += [hi, lo, hi]
        rhs = jnp.concatenate(columns, axis=0)
        r = jnp.dot(w3_ref[half], rhs, preferred_element_type=F32)
        for ri in range(2):
            for part in range(2):
                value = r[ri * 32 : ri * 32 + 32, part * 128 : part * 128 + 128]
                value = jnp.where(inside, value, 0.0)
                for z, at in enumerate(chip_rows(o, part * 2 + ri)):
                    os[at, :] = value[z * 16 : z * 16 + 16]
    out_ref[...] = os[...].astype(BF16)


VMEM = pl.BlockSpec(memory_space=pltpu.VMEM)
SMEM = pl.BlockSpec(memory_space=pltpu.SMEM)
HBM = pl.BlockSpec(memory_space=pltpu.HBM)


def call(kernel, name, inputs, outs, scratch, spaces=None, to=None):
    specs = spaces or [SMEM if x.ndim == 1 else VMEM for x in inputs]
    single = len(outs) == 1
    out = pl.pallas_call(
        kernel,
        name=name,
        out_shape=[jax.ShapeDtypeStruct(s, d) for s, d in outs],
        in_specs=specs,
        out_specs=[to or VMEM for o in outs],
        scratch_shapes=scratch,
        compiler_params=pltpu.CompilerParams(vmem_limit_bytes=48 << 20),
    )(*inputs)
    return out[0] if single else out


def in_hbm(x):
    return pltpu.with_memory_space_constraint(x, pltpu.HBM)


def scratch(shape, dtype=F32):
    return pltpu.VMEM(shape, dtype)


def body(emode_coeffs, lensing_coeffs, order_values, circle_indices, circle_weights):
    const = {k: jnp.asarray(v) for k, v in CONST.items()}
    sent, orders = call(
        pack_kernel,
        "pack",
        [
            in_hbm(emode_coeffs.reshape(512, 128)),
            in_hbm(lensing_coeffs.reshape(512, 128)),
            in_hbm(order_values),
        ],
        [((2048, 128), BF16), ((32,), jnp.int32)],
        [
            scratch((2, 512, 128), BF16),
            scratch((2, 512, 128)),
            scratch((1024, 128)),
            pltpu.SemaphoreType.DMA((3,)),
        ],
        [HBM] * 3,
    )
    fourier, fourier_t, weights = call(
        table_kernel,
        "tables",
        [orders, circle_indices.reshape(32, 128), circle_weights.reshape(32, 128)],
        [((2, 64, LONGS), BF16), ((2, LONGS, 64), BF16), ((8, 128), F32)],
        [],
    )
    got = lax.all_to_all(sent.reshape(128, 16, 128), CHIPS, 0, 0, tiled=True)
    kept, passed = call(
        synth_kernel,
        "synth",
        [orders, got.reshape(2048, 128), const["w1"], const["tw"], const["w2"]],
        [((256, 768), BF16)] * 2,
        [scratch((2048, 128)), scratch((6, 512, 128))],
    )
    held, handed = call(
        pixel_kernel,
        "pixel",
        [kept, swap_cores(passed), fourier, fourier_t, weights],
        [((256, 256), BF16)] * 2,
        [],
    )
    sums = call(
        adjoint_kernel,
        "adjoint",
        [orders, held, swap_cores(handed), const["tw"], const["wadj"], const["w3"]],
        [((2048, 128), BF16)],
        [scratch((2, 512, 128)), scratch((2048, 128))],
    )
    home = lax.all_to_all(sums.reshape(128, 16, 128), CHIPS, 0, 0, tiled=True)
    grad, curl = call(
        unpack_kernel,
        "unpack",
        [home.reshape(2048, 128)],
        [((512, 128), BF16), ((512, 128), BF16)],
        [
            scratch((1024, 128)),
            scratch((2, 512, 128)),
            scratch((2, 512, 128), BF16),
            pltpu.SemaphoreType.DMA((2,)),
        ],
        to=HBM,
    )
    return grad.reshape(128, ORD_DEV, 128), curl.reshape(128, ORD_DEV, 128)


def solution(mesh):
    split = Mesh(mesh.devices.reshape(4, 2, 4, 4, 2), ALL)
    placed = P(("y", "x", "z"), ("row", "core"), None)
    return jax.shard_map(
        body,
        mesh=split,
        in_specs=(placed, placed, P(), P(), P()),
        out_specs=(placed, placed),
        check_vma=False,
    )
```
